256 devices in a mesh: az: 64 (over x, z, core), rg: 4 (over y).
Axes of the slice: x: 4, y: 4, z: 8, core: 2. Of those that a mesh axis runs over, the one named last changes fastest.
Arguments:
- echoes: bfloat16 [2, 2048, 32768], P(None, 'rg', 'az'), may hold values from -6 to 6
- coef_table: bfloat16 [8, 5, 128, 128], replicated, may hold values from -0.3125 to 0.3125
- kern_id: int32 [256], replicated, may hold values from 0 to 7
- band_lo: int32 [256], replicated, may hold values from -2 to 2, as said below
- band_width: int32 [256], replicated, may hold values from 1 to 5
- rate: float32 [2048], P('rg'), may hold values from 4 to 40
Outputs:
- image: bfloat16 [2, 2048, 32768], P(None, ('rg', 'az'))
The draws below stay inside these ranges and needn't reach their ends.
Inputs may be any that keep to these rules, and one draw needn't show every extreme that they name: band_lo[b] + band_width[b] - 1 <= 2 for every frequency block b.
All inputs are finite; a program needn't handle non-finite values.
Results may differ from the reference program's by a relative error of at most 0.0095.
Values may be sent and summed in bfloat16 or wider, within the bound.
No kernel may reach another device: no remote copies, remote signals or barrier semaphores. Data moves between devices by JAX's collectives and lax.ppermute only.
A program may use at most 64 MiB of HBM per device.

```python
import math
import jax
import jax.numpy as jnp
from jax import lax

A = 32768
P_SIZE = 512
Q = 64
R = 2048
TILE = 128
FB = 128
FBLK = 256
HT = 2
WMAX = 5
NKER = 8


def band_draw(key):
    blocks = lax.broadcasted_iota(jnp.int32, (FBLK,), 0)
    half = FBLK // 2
    placed = jnp.minimum(blocks, FBLK - 1 - blocks)
    growth = placed * placed * WMAX // (half * half)
    jitter = jax.random.randint(jax.random.fold_in(key, 11), (FBLK,), -1, 2)
    pinned = (placed == 0) | (placed == half - 1)
    jitter = jnp.where(pinned, 0, jitter)
    width = jnp.clip(1 + growth + jitter, 1, WMAX)
    spaces = 2 * HT + 2 - width
    picked = jax.random.randint(jax.random.fold_in(key, 12), (FBLK,), 0, 1 << 20) % spaces
    lower = picked - HT
    lower = jnp.where(blocks == 0, HT + 1 - width, lower)
    return (lower.astype(jnp.int32), width.astype(jnp.int32))


def draw_band_lo(key, part):
    return band_draw(key)[0]


def draw_band_width(key, part):
    return band_draw(key)[1]


def place_ends(values, key, smallest, high):
    dims = values.shape
    spot = [jax.random.randint(jax.random.fold_in(key, axis), (), 0, dims[axis]) for axis in range(len(dims))]
    values = values.at[tuple(spot)].set(smallest)
    longest = dims.index(max(dims))
    spot[longest] = (spot[longest] + 1) % dims[longest]
    return values.at[tuple(spot)].set(high)


def steps_of(stream_key, shape, cuts, least, high):
    gain = 1.0
    for position, blocks in cuts:
        heights = jax.random.uniform(jax.random.fold_in(jax.random.fold_in(stream_key, 6), position), (blocks,), jnp.float32, least / len(cuts), high / len(cuts))
        gain = gain * jnp.repeat(jnp.exp(heights), shape[position] // blocks).reshape((-1,) + (1,) * (len(shape) - 1 - position))
    return gain


def normal_values(key, shape, spread, bound, cuts=(), dtype=jnp.bfloat16):
    entries = jax.random.normal(key, shape, jnp.float32) * spread
    if len(cuts) > 0:
        entries = steps_of(key, shape, cuts, -0.22, 0.18) * entries
    return jnp.clip(entries, min=-bound, max=bound).astype(dtype)


def setup_inputs(seed: int = 0) -> dict:
    arg_keys = jax.random.split(jax.random.key(seed), 7)
    return {
        "echoes": normal_values(arg_keys[0], (2, R, A), 1.0, 6.0, ((1, 4), (2, 64))),
        "coef_table": normal_values(arg_keys[1], (NKER, WMAX, TILE, TILE), (3 * TILE) ** -0.5, 0.3125),
        "kern_id": place_ends(jax.random.randint(arg_keys[2], (FBLK,), 0, NKER), jax.random.fold_in(arg_keys[2], 1), 0, NKER - 1).astype(jnp.int32),
        "band_lo": draw_band_lo(jax.random.fold_in(arg_keys[6], 71), 0),
        "band_width": draw_band_width(jax.random.fold_in(arg_keys[6], 71), 0),
        "rate": jnp.clip(jnp.exp(math.log(40.0) - 2.3025851 * jax.random.uniform(arg_keys[5], (R,), jnp.float32) ** steps_of(arg_keys[5], (R,), ((0, 4),), -0.2, 0.2)), 4.0, 40.0),
    }


PRECISE = lax.Precision.HIGHEST
TWO_PI = 2.0 * math.pi

def rotation(first, second, length):
    product = lax.broadcasted_iota(jnp.int32, (first, second), 0) * lax.broadcasted_iota(jnp.int32, (first, second), 1)
    angle = (product % length).astype(jnp.float32) * (TWO_PI / length)
    return (jnp.cos(angle), jnp.sin(angle))

def tables():
    cosine_first, sine_first = rotation(P_SIZE, P_SIZE, P_SIZE)
    cosine_second, sine_second = rotation(Q, Q, Q)
    cosine_twist, sine_twist = rotation(Q, P_SIZE, A)
    scale_first = 1.0 / math.sqrt(P_SIZE)
    scale_second = 1.0 / math.sqrt(Q)
    return ((cosine_first * scale_first).astype(jnp.bfloat16), (sine_first * scale_first).astype(jnp.bfloat16), (cosine_second * scale_second).astype(jnp.bfloat16), (sine_second * scale_second).astype(jnp.bfloat16), cosine_twist, sine_twist)

def contract(form, left, right):
    return jnp.einsum(form, left.astype(jnp.float32), right.astype(jnp.float32), precision=PRECISE)

def forward(planes, factors):
    cosine_first, sine_first, cosine_second, sine_second, cosine_twist, sine_twist = factors
    width = planes.shape[1]
    grid = planes.reshape(2, width, P_SIZE, Q)
    real_part = grid[0]
    imaginary = grid[1]
    first_real = contract('cpq,pf->cqf', real_part, cosine_first) + contract('cpq,pf->cqf', imaginary, sine_first)
    first_imaginary = contract('cpq,pf->cqf', imaginary, cosine_first) - contract('cpq,pf->cqf', real_part, sine_first)
    turned_real = (first_real * cosine_twist + first_imaginary * sine_twist).astype(jnp.bfloat16)
    turned_imaginary = (first_imaginary * cosine_twist - first_real * sine_twist).astype(jnp.bfloat16)
    second_real = contract('gq,cqf->cgf', cosine_second, turned_real) + contract('gq,cqf->cgf', sine_second, turned_imaginary)
    second_imaginary = contract('gq,cqf->cgf', cosine_second, turned_imaginary) - contract('gq,cqf->cgf', sine_second, turned_real)
    return jnp.stack([second_real, second_imaginary]).reshape(2, width, A).astype(jnp.bfloat16)

def inverse(planes, factors):
    cosine_first, sine_first, cosine_second, sine_second, cosine_twist, sine_twist = factors
    width = planes.shape[1]
    grid = planes.reshape(2, width, Q, P_SIZE)
    real_part = grid[0]
    imaginary = grid[1]
    first_real = contract('qg,cgf->cqf', cosine_second, real_part) - contract('qg,cgf->cqf', sine_second, imaginary)
    first_imaginary = contract('qg,cgf->cqf', cosine_second, imaginary) + contract('qg,cgf->cqf', sine_second, real_part)
    turned_real = (first_real * cosine_twist - first_imaginary * sine_twist).astype(jnp.bfloat16)
    turned_imaginary = (first_imaginary * cosine_twist + first_real * sine_twist).astype(jnp.bfloat16)
    second_real = contract('cqf,fp->cpq', turned_real, cosine_first) - contract('cqf,fp->cpq', turned_imaginary, sine_first)
    second_imaginary = contract('cqf,fp->cpq', turned_imaginary, cosine_first) + contract('cqf,fp->cpq', turned_real, sine_first)
    return jnp.stack([second_real, second_imaginary]).reshape(2, width, A).astype(jnp.bfloat16)

def migrate(spectrum, coef_table, kern_id, band_lo, band_width, rate):
    rim = HT * TILE
    padded = jnp.pad(spectrum, ((0, 0), (rim, rim), (0, 0)))
    blocks = padded.reshape(2, R + 2 * rim, FBLK, FB).transpose(2, 0, 1, 3)
    signed = (lax.broadcasted_iota(jnp.int32, (A,), 0) + A // 2) % A - A // 2
    doppler = signed.astype(jnp.float32) / A
    squared = (doppler * doppler).reshape(FBLK, FB)

    def one_block(inputs):
        columns, lower, width, kernel_index, squared_block = inputs
        kernel = coef_table[kernel_index]
        total = jnp.zeros((2, R // TILE, TILE, FB), jnp.float32)
        for offset in range(WMAX):
            start = ((HT + lower + offset) * TILE).astype(jnp.int32)
            slab = lax.dynamic_slice_in_dim(columns, start, R, 1).reshape(2, R // TILE, TILE, FB)
            weight = jnp.where(offset < width, kernel[offset], jnp.zeros_like(kernel[offset]))
            total = total + contract('ij,ptjf->ptif', weight, slab)
        moved = total.reshape(2, R, FB)
        phase = rate[:, None] * squared_block[None, :] * TWO_PI
        cosine = jnp.cos(phase)
        sine = jnp.sin(phase)
        focused_real = moved[0] * cosine + moved[1] * sine
        focused_imaginary = moved[1] * cosine - moved[0] * sine
        return jnp.stack([focused_real, focused_imaginary]).astype(jnp.bfloat16)
    result = lax.map(one_block, (blocks, band_lo, band_width, kern_id, squared))
    return result.transpose(1, 2, 0, 3).reshape(2, R, A)

def reference(echoes, coef_table, kern_id, band_lo, band_width, rate):
    factors = tables()
    group = 256

    def forward_group(block):
        return forward(block, factors)

    def inverse_group(block):
        return inverse(block, factors)
    stacked = echoes.reshape(2, R // group, group, A).transpose(1, 0, 2, 3)
    spectrum = lax.map(forward_group, stacked).transpose(1, 0, 2, 3).reshape(2, R, A)
    focused = migrate(spectrum, coef_table, kern_id, band_lo, band_width, rate)
    stacked = focused.reshape(2, R // group, group, A).transpose(1, 0, 2, 3)
    image = lax.map(inverse_group, stacked).transpose(1, 0, 2, 3).reshape(2, R, A)
    return image
```

```python
import functools
import math

import jax
import jax.numpy as jnp
import ml_dtypes
import numpy as np
from jax import lax
from jax.experimental import pallas as pl
from jax.experimental.pallas import tpu as pltpu
from jax.sharding import PartitionSpec as P

A = 32768
P_SIZE = 512
Q = 64
R = 2048
TILE = 128
FB = 128
FBLK = 256
HT = 2
WMAX = 5
ROWS = 8
HALF = 64
LIMIT = 48 * 1024 * 1024


def angles(first, second, length):
    product = np.outer(np.arange(first), np.arange(second)) % length
    turn = product * (2.0 * math.pi / length)
    return np.cos(turn), np.sin(turn)


def rounded(values):
    return values.astype(np.float32).astype(ml_dtypes.bfloat16)


@functools.lru_cache(maxsize=None)
def tables():
    cosine, sine = angles(P_SIZE, P_SIZE, P_SIZE)
    cosine, sine = cosine / math.sqrt(P_SIZE), sine / math.sqrt(P_SIZE)
    whole = np.zeros((2, P_SIZE, 2, P_SIZE))
    whole[0, :, 0] = cosine
    whole[0, :, 1] = sine
    whole[1, :, 1] = cosine
    whole[1, :, 0] = -sine
    first = whole.reshape(2, 4, 128, 2, 64, 4, 2).transpose(1, 0, 2, 4, 6, 3, 5).reshape(1024, 1024)
    back = np.zeros((2, P_SIZE, 2, P_SIZE))
    back[0, :, 0] = cosine
    back[0, :, 1] = -sine
    back[1, :, 1] = cosine
    back[1, :, 0] = sine
    last = back.reshape(2, 2, 128, 2, 2, P_SIZE).transpose(0, 1, 3, 2, 4, 5).reshape(1024, 1024)
    cosine, sine = angles(Q, Q, Q)
    cosine, sine = cosine / math.sqrt(Q), sine / math.sqrt(Q)
    eye = np.eye(ROWS)
    small = np.zeros((2, Q, 2, Q))
    small[0, :, 0] = cosine
    small[0, :, 1] = sine
    small[1, :, 1] = cosine
    small[1, :, 0] = -sine
    second = np.einsum("pgqa,rs->gprqsa", small, eye).reshape(1024, 1024)
    small = np.zeros((2, Q, 2, Q))
    small[0, :, 0] = cosine
    small[0, :, 1] = -sine
    small[1, :, 1] = cosine
    small[1, :, 0] = sine
    third = np.einsum("paqg,rs->rpagqs", small, eye)
    third = third.reshape(4, 2, 2, Q, Q, 2, ROWS).transpose(0, 2, 1, 3, 4, 5, 6).reshape(1024, 1024)
    cosine, sine = angles(Q, P_SIZE, A)
    turned = [np.tile(part.T, (1, 2)).astype(np.float32) for part in (cosine, sine)]
    straight = [np.tile(part, (2, 1)).astype(np.float32) for part in (cosine, sine)]
    return (rounded(first), rounded(second), *turned), (rounded(third), rounded(last), *straight)


def pack_kernel(echo_ref, out_ref, stage):
    low = lax.broadcasted_iota(jnp.int32, (8, 128), 1) < HALF
    for dest in range(echo_ref.shape[1] // ROWS):
        for plane in range(2):
            rows = echo_ref[plane, dest * ROWS : (dest + 1) * ROWS, :].astype(jnp.float32)
            for part in range(4):
                stage[pl.ds((dest * 8 + plane * 4 + part) * 8, 8), :] = rows[:, part * 128 : (part + 1) * 128]
    for dest in range(echo_ref.shape[1] // ROWS):
        for pair in range(4):
            even = stage[pl.ds(dest * 64 + 2 * pair, 8, stride=8), :]
            odd = stage[pl.ds(dest * 64 + 2 * pair + 1, 8, stride=8), :]
            lower = jnp.where(low, even, pltpu.roll(odd, HALF, 1))
            upper = jnp.where(low, pltpu.roll(even, HALF, 1), odd)
            both = jnp.concatenate([lower, upper], axis=0).astype(jnp.bfloat16)
            out_ref[dest, :, pair * 128 : (pair + 1) * 128] = both


def pack(echoes):
    steps = 4
    rows = 512 // steps
    return pl.pallas_call(
        pack_kernel,
        grid=(steps,),
        in_specs=[pl.BlockSpec((2, rows, 512), lambda i: (0, i, 0))],
        out_specs=pl.BlockSpec((rows // ROWS, 16, 512), lambda i: (i, 0, 0)),
        out_shape=jax.ShapeDtypeStruct((64, 16, 512), jnp.bfloat16),
        scratch_shapes=[pltpu.VMEM((rows * 8, 128), jnp.float32)],
        compiler_params=pltpu.CompilerParams(vmem_limit_bytes=LIMIT),
        name="pack",
    )(echoes)


def forward_kernel(x_ref, first_ref, second_ref, cos_ref, sin_ref, out_ref, turned):
    for chunk in range(4):
        sums = jnp.dot(
            first_ref[chunk * 256 : (chunk + 1) * 256, :], x_ref[...], preferred_element_type=jnp.float32
        )
        cosine = cos_ref[chunk * 128 : (chunk + 1) * 128, :]
        sine = sin_ref[chunk * 128 : (chunk + 1) * 128, :]
        for pair in range(4):
            real = sums[:128, pair * 128 : (pair + 1) * 128]
            imaginary = sums[128:, pair * 128 : (pair + 1) * 128]
            span = slice(chunk * 128, (chunk + 1) * 128)
            turned[span, pair * 128 : (pair + 1) * 128] = (real * cosine + imaginary * sine).astype(jnp.bfloat16)
            turned[span, 512 + pair * 128 : 512 + (pair + 1) * 128] = (
                imaginary * cosine - real * sine
            ).astype(jnp.bfloat16)
    for chunk in range(4):
        sums = lax.dot_general(
            second_ref[chunk * 256 : (chunk + 1) * 256, :],
            turned[...],
            (((1,), (1,)), ((), ())),
            preferred_element_type=jnp.float32,
        ).astype(jnp.bfloat16)
        for part in range(4):
            out_ref[chunk * 16 : (chunk + 1) * 16, part] = sums[:, part * 128 : (part + 1) * 128].reshape(16, 16, 128)


def forward(x, first, second, cosine, sine):
    return pl.pallas_call(
        forward_kernel,
        out_shape=jax.ShapeDtypeStruct((64, 4, 16, 128), jnp.bfloat16),
        in_specs=[pl.BlockSpec(memory_space=pltpu.VMEM)] * 5,
        out_specs=pl.BlockSpec(memory_space=pltpu.VMEM),
        scratch_shapes=[pltpu.VMEM((512, 1024), jnp.bfloat16)],
        compiler_params=pltpu.CompilerParams(vmem_limit_bytes=LIMIT),
        name="forward",
    )(x, first, second, cosine, sine)


def migrate_kernel(band_ref, spectrum_ref, coef_ref, out_ref, taps, padded):
    lower = band_ref[1]
    width = band_ref[2]
    empty = jnp.zeros((TILE, TILE), jnp.bfloat16)
    taps[:TILE, 5 * TILE :] = empty
    taps[TILE:, :TILE] = empty
    for shift in range(WMAX):
        index = shift - HT - lower
        held = jnp.logical_and(index >= 0, index < width)
        weight = coef_ref[0, jnp.clip(index, 0, WMAX - 1)]
        scale = jnp.where(held, jnp.float32(1), jnp.float32(0))
        weight = (weight.astype(jnp.float32) * scale).astype(jnp.bfloat16)
        taps[:TILE, shift * TILE : (shift + 1) * TILE] = weight
        taps[TILE:, (shift + 1) * TILE : (shift + 2) * TILE] = weight
    rim = jnp.zeros((HT * TILE, 2 * FB), jnp.bfloat16)
    padded[: HT * TILE, :] = rim
    padded[HT * TILE + R :, :] = rim
    for block in range(8):
        values = spectrum_ref[block * 32 : (block + 1) * 32].astype(jnp.float32)
        start = HT * TILE + block * 256
        for plane in range(2):
            rows = values[:, plane * ROWS : (plane + 1) * ROWS, :].reshape(256, FB)
            padded[start : start + 256, plane * FB : (plane + 1) * FB] = rows.astype(jnp.bfloat16)
    for block in range(8):
        moved = jnp.dot(
            taps[...], padded[block * 256 : block * 256 + 6 * TILE, :], preferred_element_type=jnp.float32
        )
        real = moved[:, :FB].reshape(32, ROWS, FB)
        imaginary = moved[:, FB:].reshape(32, ROWS, FB)
        out_ref[block * 32 : (block + 1) * 32] = jnp.concatenate([real, imaginary], axis=1).astype(jnp.bfloat16)


def migrate(band, spectrum, coef_table):
    return pl.pallas_call(
        migrate_kernel,
        grid_spec=pltpu.PrefetchScalarGridSpec(
            num_scalar_prefetch=1,
            grid=(1,),
            in_specs=[
                pl.BlockSpec((256, 16, 128), lambda i, band: (0, 0, 0)),
                pl.BlockSpec((1, WMAX, TILE, TILE), lambda i, band: (band[0], 0, 0, 0)),
            ],
            out_specs=pl.BlockSpec((256, 16, 128), lambda i, band: (0, 0, 0)),
            scratch_shapes=[
                pltpu.VMEM((256, 6 * TILE), jnp.bfloat16),
                pltpu.VMEM((R + 2 * HT * TILE, 2 * FB), jnp.bfloat16),
            ],
        ),
        out_shape=jax.ShapeDtypeStruct((256, 16, 128), jnp.bfloat16),
        compiler_params=pltpu.CompilerParams(vmem_limit_bytes=LIMIT),
        name="migrate",
    )(band, spectrum, coef_table)


def rotor(turns):
    quarter = jnp.round(turns * 4.0)
    x = (turns - quarter * 0.25) * (2.0 * math.pi)
    square = x * x
    sine = x + x * square * (-1.0 / 6 + square * (1.0 / 120 + square * (-1.0 / 5040)))
    cosine = 1.0 + square * (-0.5 + square * (1.0 / 24 + square * (-1.0 / 720 + square * (1.0 / 40320))))
    count = quarter.astype(jnp.int32)
    swapped = (count & 1) == 1
    first = jnp.where(swapped, sine, cosine)
    second = jnp.where(swapped, cosine, sine)
    first = jnp.where(((count + 1) & 2) == 2, -first, first)
    second = jnp.where((count & 2) == 2, -second, second)
    return first, second


def inverse_kernel(moved_ref, rate_ref, third_ref, last_ref, cos_ref, sin_ref, out_ref, focused, turned, stage):
    rate = rate_ref[...]
    lane = lax.broadcasted_iota(jnp.int32, (16, ROWS, FB), 2)
    step = lax.broadcasted_iota(jnp.int32, (16, ROWS, FB), 0)
    for chunk in range(4):
        for part in range(4):
            frequency = (step + chunk * 16) * P_SIZE + (lane + part * FB)
            signed = jnp.where(frequency >= A // 2, frequency - A, frequency).astype(jnp.float32)
            doppler = signed * (1.0 / A)
            cosine, sine = rotor(rate[None] * (doppler * doppler))
            values = moved_ref[chunk * 16 : (chunk + 1) * 16, part].astype(jnp.float32)
            real, imaginary = values[:, :ROWS, :], values[:, ROWS:, :]
            both = jnp.concatenate(
                [real * cosine + imaginary * sine, imaginary * cosine - real * sine], axis=1
            ).astype(jnp.bfloat16)
            focused[chunk * 256 : (chunk + 1) * 256, part * FB : (part + 1) * FB] = both.reshape(256, FB)
    for chunk in range(4):
        sums = jnp.dot(
            third_ref[chunk * 256 : (chunk + 1) * 256, :], focused[...], preferred_element_type=jnp.float32
        )
        real, imaginary = sums[:128], sums[128:]
        cosine, sine = cos_ref[...], sin_ref[...]
        span = slice(chunk * 128, (chunk + 1) * 128)
        turned[span, :512] = (real * cosine - imaginary * sine).astype(jnp.bfloat16)
        turned[span, 512:] = (imaginary * cosine + real * sine).astype(jnp.bfloat16)
    low = lax.broadcasted_iota(jnp.int32, (128, 128), 1) < HALF
    for chunk in range(4):
        sums = lax.dot_general(
            last_ref[chunk * 256 : (chunk + 1) * 256, :],
            turned[...],
            (((1,), (1,)), ((), ())),
            preferred_element_type=jnp.float32,
        )
        for pair in range(4):
            even = sums[:128, pair * 128 : (pair + 1) * 128]
            odd = sums[128:, pair * 128 : (pair + 1) * 128]
            stage[pl.ds(2 * pair, 128, stride=8), :] = jnp.where(low, even, pltpu.roll(odd, HALF, 1))
            stage[pl.ds(2 * pair + 1, 128, stride=8), :] = jnp.where(low, pltpu.roll(even, HALF, 1), odd)
        plane, base = chunk // 2, (chunk % 2) * 128
        for group in range(128):
            out_ref[plane, :, (base + group) * 128 : (base + group + 1) * 128] = stage[
                group * 8 : (group + 1) * 8, :
            ].astype(jnp.bfloat16)


def inverse(moved, rate, third, last, cosine, sine):
    return pl.pallas_call(
        inverse_kernel,
        out_shape=jax.ShapeDtypeStruct((2, ROWS, A), jnp.bfloat16),
        in_specs=[pl.BlockSpec(memory_space=pltpu.VMEM)] * 6,
        out_specs=pl.BlockSpec(memory_space=pltpu.VMEM),
        scratch_shapes=[
            pltpu.VMEM((1024, 512), jnp.bfloat16),
            pltpu.VMEM((512, 1024), jnp.bfloat16),
            pltpu.VMEM((1024, 128), jnp.float32),
        ],
        compiler_params=pltpu.CompilerParams(vmem_limit_bytes=LIMIT),
        name="inverse",
    )(moved, rate, third, last, cosine, sine)


def body(echoes, coef_table, kern_id, band_lo, band_width, rate):
    ahead, behind = tables()
    az = lax.axis_index("az")
    block = lax.axis_index("rg") * lax.axis_size("az") + az
    band = jnp.stack([kern_id[block], band_lo[block], band_width[block]])
    rates = jnp.broadcast_to(lax.dynamic_slice(rate, (az * ROWS,), (ROWS,))[:, None], (ROWS, FB))
    piece = lax.all_to_all(pack(echoes), "az", 0, 0, tiled=True)
    spectrum = forward(piece.reshape(1024, 512), *ahead)
    spectrum = lax.all_to_all(spectrum.reshape(256, 16, 128), ("rg", "az"), 0, 0, tiled=True)
    moved = migrate(band, spectrum, coef_table)
    moved = lax.all_to_all(moved, ("rg", "az"), 0, 0, tiled=True)
    return inverse(moved.reshape(64, 4, 16, 128), rates, *behind)


def solution(mesh):
    in_specs = (P(None, "rg", "az"), P(), P(), P(), P(), P("rg"))
    out_specs = P(None, ("rg", "az"), None)
    return jax.shard_map(body, mesh=mesh, in_specs=in_specs, out_specs=out_specs, check_vma=False)
```

```python
import functools
import math

import jax
import jax.numpy as jnp
import ml_dtypes
import numpy as np
from jax import lax
from jax.experimental import pallas as pl
from jax.experimental.pallas import tpu as pltpu
from jax.sharding import PartitionSpec as P

A = 32768
P_SIZE = 512
Q = 64
R = 2048
TILE = 128
FB = 128
FBLK = 256
HT = 2
WMAX = 5
ROWS = 8
PACKS = 8
HALF = 64
MIB = 1024 * 1024
FAR = pltpu.MemorySpace.HBM
NEAR = pltpu.MemorySpace.VMEM


def angles(first, second, length):
    product = np.outer(np.arange(first), np.arange(second)) % length
    turn = product * (2.0 * math.pi / length)
    return np.cos(turn), np.sin(turn)


def rounded(values):
    return values.astype(np.float32).astype(ml_dtypes.bfloat16)


@functools.lru_cache(maxsize=None)
def tables():
    cosine, sine = angles(P_SIZE, P_SIZE, P_SIZE)
    cosine, sine = cosine / math.sqrt(P_SIZE), sine / math.sqrt(P_SIZE)
    whole = np.zeros((2, P_SIZE, 2, P_SIZE))
    whole[0, :, 0] = cosine
    whole[0, :, 1] = sine
    whole[1, :, 1] = cosine
    whole[1, :, 0] = -sine
    first = whole.reshape(2, 4, 128, 2, 64, 4, 2).transpose(1, 0, 2, 4, 6, 3, 5).reshape(1024, 1024)
    back = np.zeros((2, P_SIZE, 2, P_SIZE))
    back[0, :, 0] = cosine
    back[0, :, 1] = -sine
    back[1, :, 1] = cosine
    back[1, :, 0] = sine
    last = back.reshape(2, 2, 128, 2, 2, P_SIZE).transpose(0, 1, 3, 2, 4, 5).reshape(1024, 1024)
    cosine, sine = angles(Q, Q, Q)
    cosine, sine = cosine / math.sqrt(Q), sine / math.sqrt(Q)
    eye = np.eye(ROWS)
    small = np.zeros((2, Q, 2, Q))
    small[0, :, 0] = cosine
    small[0, :, 1] = sine
    small[1, :, 1] = cosine
    small[1, :, 0] = -sine
    second = np.einsum("pgqa,rs->gprqsa", small, eye).reshape(1024, 1024)
    small = np.zeros((2, Q, 2, Q))
    small[0, :, 0] = cosine
    small[0, :, 1] = -sine
    small[1, :, 1] = cosine
    small[1, :, 0] = sine
    third = np.einsum("paqg,rs->rpagqs", small, eye)
    third = third.reshape(4, 2, 2, Q, Q, 2, ROWS).transpose(0, 2, 1, 3, 4, 5, 6).reshape(1024, 1024)
    cosine, sine = angles(Q, P_SIZE, A)
    turned = np.stack([np.tile(part.T, (1, 2)) for part in (cosine, sine)]).astype(np.float32)
    straight = [np.tile(part, (2, 1)).reshape(128, 4, 128).transpose(1, 0, 2).reshape(512, 128) for part in (cosine, sine)]
    straight = np.concatenate([np.stack(straight), turned, turned, turned]).astype(np.float32)
    return (rounded(first), rounded(second), turned), (rounded(third), rounded(last), straight)


def pack_kernel(echo_ref, out_ref, echo, stage, arrived):
    low = lax.broadcasted_iota(jnp.int32, (8, 128), 1) < HALF
    copies = []
    for step in range(PACKS):
        rows = pl.ds(step * (512 // PACKS), 512 // PACKS)
        copies.append(pltpu.make_async_copy(echo_ref.at[:, rows, :], echo.at[:, rows, :], arrived.at[step]))
        copies[-1].start()
    for dest in range(64):
        if dest % (64 // PACKS) == 0:
            copies[dest // (64 // PACKS)].wait()
        for plane in range(2):
            rows = echo[plane, dest * ROWS : (dest + 1) * ROWS, :].astype(jnp.float32)
            for part in range(4):
                stage[pl.ds((dest * 8 + plane * 4 + part) * 8, 8), :] = rows[:, part * 128 : (part + 1) * 128]
        for pair in range(4):
            even = stage[pl.ds(dest * 64 + 2 * pair, 8, stride=8), :]
            odd = stage[pl.ds(dest * 64 + 2 * pair + 1, 8, stride=8), :]
            lower = jnp.where(low, even, pltpu.roll(odd, HALF, 1))
            upper = jnp.where(low, pltpu.roll(even, HALF, 1), odd)
            both = jnp.concatenate([lower, upper], axis=0).astype(jnp.bfloat16)
            out_ref[dest, :, pair * 128 : (pair + 1) * 128] = both


def pack(echoes):
    return pl.pallas_call(
        pack_kernel,
        in_specs=[pl.BlockSpec(memory_space=FAR)],
        out_specs=pl.BlockSpec(memory_space=NEAR),
        out_shape=jax.ShapeDtypeStruct((64, 16, 512), jnp.bfloat16),
        scratch_shapes=[
            pltpu.VMEM((2, 512, 512), jnp.bfloat16),
            pltpu.VMEM((4096, 128), jnp.float32),
            pltpu.SemaphoreType.DMA((PACKS,)),
        ],
        compiler_params=pltpu.CompilerParams(vmem_limit_bytes=53 * MIB),
        name="pack",
    )(echoes)


def fetch(source, target, arrived, steps):
    copies = []
    rows = source.shape[0] // steps
    for step in range(steps):
        span = pl.ds(step * rows, rows)
        copies.append(pltpu.make_async_copy(source.at[span], target.at[span], arrived.at[step]))
    return copies


def forward_kernel(
    x_ref, first_ref, second_ref, twist_ref, out_ref, first, second, twist, turned, sums, out, came, went
):
    lead = fetch(first_ref, first, came.at[0], 4)
    turns = fetch(twist_ref, twist, came.at[1], 1)
    follow = fetch(second_ref, second, came.at[2], 4)
    for copy in lead[:2] + turns:
        copy.start()
    later = [lead[2:3], lead[3:], follow[:2], follow[2:]]
    for chunk in range(4):
        lead[chunk].wait()
        for copy in later[chunk]:
            copy.start()
        sums[...] = jnp.dot(
            first[chunk * 256 : (chunk + 1) * 256, :], x_ref[...], preferred_element_type=jnp.float32
        )
        if chunk == 0:
            turns[0].wait()
        span = slice(chunk * 128, (chunk + 1) * 128)
        cosine, sine = twist[0, span, :], twist[1, span, :]
        for pair in range(4):
            lanes = slice(pair * 128, (pair + 1) * 128)
            real, imaginary = sums[:128, lanes], sums[128:, lanes]
            turned[span, pair * 128 : (pair + 1) * 128] = (real * cosine + imaginary * sine).astype(jnp.bfloat16)
            turned[span, 512 + pair * 128 : 640 + pair * 128] = (imaginary * cosine - real * sine).astype(
                jnp.bfloat16
            )
    sent = []
    for chunk in range(4):
        follow[chunk].wait()
        sums[...] = lax.dot_general(
            second[chunk * 256 : (chunk + 1) * 256, :],
            turned[...],
            (((1,), (1,)), ((), ())),
            preferred_element_type=jnp.float32,
        )
        span = slice(chunk * 16, (chunk + 1) * 16)
        for part in range(4):
            values = sums[:, part * 128 : (part + 1) * 128].astype(jnp.bfloat16)
            out[span, part] = values.reshape(16, 16, 128)
        rows = pl.ds(chunk * 16, 16)
        sent.append(pltpu.make_async_copy(out.at[rows], out_ref.at[rows], went.at[chunk]))
        sent[-1].start()
    for copy in sent:
        copy.wait()


def forward(x, first, second, twist):
    return pl.pallas_call(
        forward_kernel,
        out_shape=jax.ShapeDtypeStruct((64, 4, 16, 128), jnp.bfloat16),
        in_specs=[pl.BlockSpec(memory_space=NEAR)] + [pl.BlockSpec(memory_space=FAR)] * 3,
        out_specs=pl.BlockSpec(memory_space=FAR),
        scratch_shapes=[
            pltpu.VMEM((1024, 1024), jnp.bfloat16),
            pltpu.VMEM((1024, 1024), jnp.bfloat16),
            pltpu.VMEM((2, 512, 128), jnp.float32),
            pltpu.VMEM((512, 1024), jnp.bfloat16),
            pltpu.VMEM((256, 512), jnp.float32),
            pltpu.VMEM((64, 4, 16, 128), jnp.bfloat16),
            pltpu.SemaphoreType.DMA((3, 4)),
            pltpu.SemaphoreType.DMA((4,)),
        ],
        compiler_params=pltpu.CompilerParams(vmem_limit_bytes=51 * MIB),
        name="forward",
    )(x, first, second, twist)


def taps_kernel(band_ref, coef_ref, taps):
    lower = band_ref[1]
    width = band_ref[2]
    empty = jnp.zeros((TILE, TILE), jnp.bfloat16)
    taps[:TILE, 5 * TILE :] = empty
    taps[TILE:, :TILE] = empty
    for shift in range(WMAX):
        index = shift - HT - lower
        held = jnp.logical_and(index >= 0, index < width)
        weight = coef_ref[0, jnp.clip(index, 0, WMAX - 1)]
        scale = jnp.where(held, jnp.float32(1), jnp.float32(0))
        weight = (weight.astype(jnp.float32) * scale).astype(jnp.bfloat16)
        taps[:TILE, shift * TILE : (shift + 1) * TILE] = weight
        taps[TILE:, (shift + 1) * TILE : (shift + 2) * TILE] = weight


def tap_matrix(band, coef_table):
    return pl.pallas_call(
        taps_kernel,
        grid_spec=pltpu.PrefetchScalarGridSpec(
            num_scalar_prefetch=1,
            grid=(1,),
            in_specs=[pl.BlockSpec((1, WMAX, TILE, TILE), lambda i, band: (band[0], 0, 0, 0))],
            out_specs=pl.BlockSpec((256, 6 * TILE), lambda i, band: (0, 0)),
        ),
        out_shape=jax.ShapeDtypeStruct((256, 6 * TILE), jnp.bfloat16),
        compiler_params=pltpu.CompilerParams(vmem_limit_bytes=16 * MIB),
        cost_estimate=pl.CostEstimate(flops=2_000_000, bytes_accessed=600_000, transcendentals=0),
        name="taps",
    )(band, coef_table)


def migrate_kernel(spectrum_ref, taps, out_ref, padded, out, went):
    rim = jnp.zeros((HT * TILE, 2 * FB), jnp.bfloat16)
    padded[: HT * TILE, :] = rim
    padded[HT * TILE + R :, :] = rim
    for block in range(8):
        values = spectrum_ref[block * 32 : (block + 1) * 32].astype(jnp.float32)
        start = HT * TILE + block * 256
        for plane in range(2):
            rows = values[:, plane * ROWS : (plane + 1) * ROWS, :].reshape(256, FB)
            padded[start : start + 256, plane * FB : (plane + 1) * FB] = rows.astype(jnp.bfloat16)
    sent = []
    for block in range(8):
        moved = jnp.dot(
            taps[...], padded[block * 256 : block * 256 + 6 * TILE, :], preferred_element_type=jnp.float32
        )
        real = moved[:, :FB].reshape(32, ROWS, FB)
        imaginary = moved[:, FB:].reshape(32, ROWS, FB)
        out[block * 32 : (block + 1) * 32] = jnp.concatenate([real, imaginary], axis=1).astype(jnp.bfloat16)
        if block % 2 == 1:
            rows = pl.ds(block * 32 - 32, 64)
            sent.append(pltpu.make_async_copy(out.at[rows], out_ref.at[rows], went.at[block // 2]))
            sent[-1].start()
    for copy in sent:
        copy.wait()


def migrate(spectrum, taps):
    return pl.pallas_call(
        migrate_kernel,
        in_specs=[pl.BlockSpec(memory_space=NEAR)] * 2,
        out_specs=pl.BlockSpec(memory_space=FAR),
        scratch_shapes=[
            pltpu.VMEM((R + 2 * HT * TILE, 2 * FB), jnp.bfloat16),
            pltpu.VMEM((256, 16, 128), jnp.bfloat16),
            pltpu.SemaphoreType.DMA((4,)),
        ],
        out_shape=jax.ShapeDtypeStruct((256, 16, 128), jnp.bfloat16),
        compiler_params=pltpu.CompilerParams(vmem_limit_bytes=50 * MIB),
        name="migrate",
    )(spectrum, taps)


def rotor(turns):
    quarter = jnp.round(turns * 4.0)
    x = (turns - quarter * 0.25) * (2.0 * math.pi)
    square = x * x
    sine = x + x * square * (-1.0 / 6 + square * (1.0 / 120 + square * (-1.0 / 5040)))
    cosine = 1.0 + square * (-0.5 + square * (1.0 / 24 + square * (-1.0 / 720 + square * (1.0 / 40320))))
    count = quarter.astype(jnp.int32)
    swapped = (count & 1) == 1
    first = jnp.where(swapped, sine, cosine)
    second = jnp.where(swapped, cosine, sine)
    first = jnp.where(((count + 1) & 2) == 2, -first, first)
    second = jnp.where((count & 2) == 2, -second, second)
    return first, second


def phase_kernel(rate_ref, phase_ref):
    rate = rate_ref[...]
    lane = lax.broadcasted_iota(jnp.int32, (16, ROWS, FB), 2)
    step = lax.broadcasted_iota(jnp.int32, (16, ROWS, FB), 0)
    for chunk in range(4):
        for part in range(4):
            frequency = (step + chunk * 16) * P_SIZE + (lane + part * FB)
            signed = jnp.where(frequency >= A // 2, frequency - A, frequency).astype(jnp.float32)
            doppler = signed * (1.0 / A)
            cosine, sine = rotor(rate[None] * (doppler * doppler))
            phase_ref[0, chunk * 16 : (chunk + 1) * 16, part] = cosine
            phase_ref[1, chunk * 16 : (chunk + 1) * 16, part] = sine


def phases(rate):
    return pl.pallas_call(
        phase_kernel,
        out_shape=jax.ShapeDtypeStruct((2, 64, 4, ROWS, FB), jnp.float32),
        in_specs=[pl.BlockSpec(memory_space=NEAR)],
        out_specs=pl.BlockSpec(memory_space=NEAR),
        compiler_params=pltpu.CompilerParams(vmem_limit_bytes=16 * MIB),
        cost_estimate=pl.CostEstimate(flops=20_000_000, bytes_accessed=2_100_000, transcendentals=0),
        name="phases",
    )(rate)


def inverse_kernel(
    moved_ref,
    phase_ref,
    third_ref,
    last_ref,
    twist_ref,
    out_ref,
    third,
    last,
    twist,
    focused,
    turned,
    sums,
    stage,
    out,
    came,
    went,
):
    lead = fetch(third_ref, third, came.at[0], 4)
    turns = fetch(twist_ref.at[:2], twist, came.at[1], 1)
    follow = fetch(last_ref, last, came.at[2], 4)
    for copy in lead[:2] + turns:
        copy.start()
    later = [lead[2:3], lead[3:], follow[:2], follow[2:]]
    for chunk in range(4):
        for part in range(4):
            span = slice(chunk * 16, (chunk + 1) * 16)
            cosine, sine = phase_ref[0, span, part], phase_ref[1, span, part]
            values = moved_ref[span, part].astype(jnp.float32)
            real, imaginary = values[:, :ROWS, :], values[:, ROWS:, :]
            both = jnp.concatenate(
                [real * cosine + imaginary * sine, imaginary * cosine - real * sine], axis=1
            ).astype(jnp.bfloat16)
            focused[chunk * 256 : (chunk + 1) * 256, part * FB : (part + 1) * FB] = both.reshape(256, FB)
    for chunk in range(4):
        lead[chunk].wait()
        for copy in later[chunk]:
            copy.start()
        if chunk == 0:
            turns[0].wait()
        sums[...] = jnp.dot(
            third[chunk * 256 : (chunk + 1) * 256, :], focused[...], preferred_element_type=jnp.float32
        )
        span = slice(chunk * 128, (chunk + 1) * 128)
        for part in range(4):
            lanes = slice(part * 128, (part + 1) * 128)
            real, imaginary = sums[:128, lanes], sums[128:, lanes]
            cosine, sine = twist[0, lanes, :], twist[1, lanes, :]
            turned[span, part * 128 : (part + 1) * 128] = (real * cosine - imaginary * sine).astype(jnp.bfloat16)
            turned[span, 512 + part * 128 : 640 + part * 128] = (imaginary * cosine + real * sine).astype(
                jnp.bfloat16
            )
    low = lax.broadcasted_iota(jnp.int32, (128, 128), 1) < HALF
    sent = []
    for chunk in range(4):
        follow[chunk].wait()
        sums[...] = lax.dot_general(
            last[chunk * 256 : (chunk + 1) * 256, :],
            turned[...],
            (((1,), (1,)), ((), ())),
            preferred_element_type=jnp.float32,
        )
        for pair in range(4):
            even = sums[:128, pair * 128 : (pair + 1) * 128]
            odd = sums[128:, pair * 128 : (pair + 1) * 128]
            stage[chunk % 2, pl.ds(2 * pair, 128, stride=8), :] = jnp.where(low, even, pltpu.roll(odd, HALF, 1))
            stage[chunk % 2, pl.ds(2 * pair + 1, 128, stride=8), :] = jnp.where(low, pltpu.roll(even, HALF, 1), odd)
        plane, base = chunk // 2, (chunk % 2) * 128
        for group in range(128):
            out[plane, :, (base + group) * 128 : (base + group + 1) * 128] = stage[
                chunk % 2, group * 8 : (group + 1) * 8, :
            ].astype(jnp.bfloat16)
        lanes = pl.ds(base * 128, A // 2)
        sent.append(pltpu.make_async_copy(out.at[plane, :, lanes], out_ref.at[plane, :, lanes], went.at[chunk]))
        sent[-1].start()
    for copy in sent:
        copy.wait()


def inverse(moved, phase, third, last, twist):
    return pl.pallas_call(
        inverse_kernel,
        out_shape=jax.ShapeDtypeStruct((2, ROWS, A), jnp.bfloat16),
        in_specs=[pl.BlockSpec(memory_space=NEAR)] * 2 + [pl.BlockSpec(memory_space=FAR)] * 3,
        out_specs=pl.BlockSpec(memory_space=FAR),
        scratch_shapes=[
            pltpu.VMEM((1024, 1024), jnp.bfloat16),
            pltpu.VMEM((1024, 1024), jnp.bfloat16),
            pltpu.VMEM((2, 512, 128), jnp.float32),
            pltpu.VMEM((1024, 512), jnp.bfloat16),
            pltpu.VMEM((512, 1024), jnp.bfloat16),
            pltpu.VMEM((256, 512), jnp.float32),
            pltpu.VMEM((2, 1024, 128), jnp.float32),
            pltpu.VMEM((2, ROWS, A), jnp.bfloat16),
            pltpu.SemaphoreType.DMA((3, 4)),
            pltpu.SemaphoreType.DMA((4,)),
        ],
        compiler_params=pltpu.CompilerParams(vmem_limit_bytes=50 * MIB),
        name="inverse",
    )(moved, phase, third, last, twist)


def body(echoes, coef_table, kern_id, band_lo, band_width, rate):
    ahead, behind = tables()
    az = lax.axis_index("az")
    block = lax.axis_index("rg") * lax.axis_size("az") + az
    band = jnp.stack([kern_id[block], band_lo[block], band_width[block]])
    rates = jnp.broadcast_to(lax.dynamic_slice(rate, (az * ROWS,), (ROWS,))[:, None], (ROWS, FB))
    piece = lax.all_to_all(pack(echoes), "az", 0, 0, tiled=True)
    spectrum = forward(piece.reshape(1024, 512), *ahead)
    spectrum = lax.all_to_all(spectrum.reshape(256, 16, 128), ("rg", "az"), 0, 0, tiled=True)
    moved = migrate(spectrum, tap_matrix(band, coef_table))
    moved = lax.all_to_all(moved, ("rg", "az"), 0, 0, tiled=True)
    return inverse(moved.reshape(64, 4, 16, 128), phases(rates), *behind)


def solution(mesh):
    in_specs = (P(None, "rg", "az"), P(), P(), P(), P(), P("rg"))
    out_specs = P(None, ("rg", "az"), None)
    return jax.shard_map(body, mesh=mesh, in_specs=in_specs, out_specs=out_specs, check_vma=False)
```

```python
import functools
import math

import jax
import jax.numpy as jnp
import ml_dtypes
import numpy as np
from jax import lax
from jax.experimental import pallas as pl
from jax.experimental.pallas import tpu as pltpu
from jax.sharding import PartitionSpec as P

A = 32768
P_SIZE = 512
Q = 64
R = 2048
TILE = 128
FB = 128
FBLK = 256
HT = 2
WMAX = 5
ROWS = 8
PACKS = 8
HALF = 64
MIB = 1024 * 1024
FAR = pltpu.MemorySpace.HBM
NEAR = pltpu.MemorySpace.VMEM


def angles(first, second, length):
    product = np.outer(np.arange(first), np.arange(second)) % length
    turn = product * (2.0 * math.pi / length)
    return np.cos(turn), np.sin(turn)


def rounded(values):
    return values.astype(np.float32).astype(ml_dtypes.bfloat16)


@functools.lru_cache(maxsize=None)
def tables():
    cosine, sine = angles(P_SIZE, P_SIZE, P_SIZE)
    cosine, sine = cosine / math.sqrt(P_SIZE), sine / math.sqrt(P_SIZE)
    whole = np.zeros((2, P_SIZE, 2, P_SIZE))
    whole[0, :, 0] = cosine
    whole[0, :, 1] = sine
    whole[1, :, 1] = cosine
    whole[1, :, 0] = -sine
    first = whole.reshape(2, 4, 128, 2, 64, 4, 2).transpose(1, 0, 2, 4, 6, 3, 5).reshape(1024, 1024)
    back = np.zeros((2, P_SIZE, 2, P_SIZE))
    back[0, :, 0] = cosine
    back[0, :, 1] = -sine
    back[1, :, 1] = cosine
    back[1, :, 0] = sine
    last = back.reshape(2, 2, 128, 2, 2, P_SIZE).transpose(0, 1, 3, 2, 4, 5).reshape(1024, 1024)
    cosine, sine = angles(Q, Q, Q)
    cosine, sine = cosine / math.sqrt(Q), sine / math.sqrt(Q)
    eye = np.eye(ROWS)
    small = np.zeros((2, Q, 2, Q))
    small[0, :, 0] = cosine
    small[0, :, 1] = sine
    small[1, :, 1] = cosine
    small[1, :, 0] = -sine
    second = np.einsum("pgqa,rs->gprqsa", small, eye).reshape(1024, 1024)
    small = np.zeros((2, Q, 2, Q))
    small[0, :, 0] = cosine
    small[0, :, 1] = -sine
    small[1, :, 1] = cosine
    small[1, :, 0] = sine
    third = np.einsum("paqg,rs->rpagqs", small, eye)
    third = third.reshape(4, 2, 2, Q, Q, 2, ROWS).transpose(0, 2, 1, 3, 4, 5, 6).reshape(1024, 1024)
    cosine, sine = angles(Q, P_SIZE, A)
    turned = np.stack([np.tile(part.T, (1, 2)) for part in (cosine, sine)]).astype(np.float32)
    straight = [np.tile(part, (2, 1)).reshape(128, 4, 128).transpose(1, 0, 2).reshape(512, 128) for part in (cosine, sine)]
    straight = np.concatenate([np.stack(straight), turned, turned, turned]).astype(np.float32)
    return (rounded(first), turned, rounded(second)), (rounded(third), rounded(last), straight)


def pack_kernel(echo_ref, out_ref, echo, stage, arrived):
    low = lax.broadcasted_iota(jnp.int32, (8, 128), 1) < HALF
    copies = []
    for step in range(PACKS):
        rows = pl.ds(step * (512 // PACKS), 512 // PACKS)
        copies.append(pltpu.make_async_copy(echo_ref.at[:, rows, :], echo.at[:, rows, :], arrived.at[step]))
        copies[-1].start()
    for dest in range(64):
        if dest % (64 // PACKS) == 0:
            copies[dest // (64 // PACKS)].wait()
        for plane in range(2):
            rows = echo[plane, dest * ROWS : (dest + 1) * ROWS, :].astype(jnp.float32)
            for part in range(4):
                stage[pl.ds((dest * 8 + plane * 4 + part) * 8, 8), :] = rows[:, part * 128 : (part + 1) * 128]
        for pair in range(4):
            even = stage[pl.ds(dest * 64 + 2 * pair, 8, stride=8), :]
            odd = stage[pl.ds(dest * 64 + 2 * pair + 1, 8, stride=8), :]
            lower = jnp.where(low, even, pltpu.roll(odd, HALF, 1))
            upper = jnp.where(low, pltpu.roll(even, HALF, 1), odd)
            both = jnp.concatenate([lower, upper], axis=0).astype(jnp.bfloat16)
            out_ref[dest, :, pair * 128 : (pair + 1) * 128] = both


def pack(echoes):
    return pl.pallas_call(
        pack_kernel,
        in_specs=[pl.BlockSpec(memory_space=FAR)],
        out_specs=pl.BlockSpec(memory_space=NEAR),
        out_shape=jax.ShapeDtypeStruct((64, 16, 512), jnp.bfloat16),
        scratch_shapes=[
            pltpu.VMEM((2, 512, 512), jnp.bfloat16),
            pltpu.VMEM((4096, 128), jnp.float32),
            pltpu.SemaphoreType.DMA((PACKS,)),
        ],
        compiler_params=pltpu.CompilerParams(vmem_limit_bytes=52 * MIB),
        name="pack",
    )(echoes)


def fetch(source, target, arrived, steps):
    copies = []
    rows = source.shape[0] // steps
    for step in range(steps):
        span = pl.ds(step * rows, rows)
        copies.append(pltpu.make_async_copy(source.at[span], target.at[span], arrived.at[step]))
    return copies


def forward_kernel(
    x_ref, first, twist, second_ref, out_ref, second, turned, sums, out, came, went
):
    follow = fetch(second_ref, second, came, 4)
    for copy in follow:
        copy.start()
    for chunk in range(4):
        sums[...] = jnp.dot(
            first[chunk * 256 : (chunk + 1) * 256, :], x_ref[...], preferred_element_type=jnp.float32
        )
        span = slice(chunk * 128, (chunk + 1) * 128)
        cosine, sine = twist[0, span, :], twist[1, span, :]
        for pair in range(4):
            lanes = slice(pair * 128, (pair + 1) * 128)
            real, imaginary = sums[:128, lanes], sums[128:, lanes]
            turned[span, pair * 128 : (pair + 1) * 128] = (real * cosine + imaginary * sine).astype(jnp.bfloat16)
            turned[span, 512 + pair * 128 : 640 + pair * 128] = (imaginary * cosine - real * sine).astype(
                jnp.bfloat16
            )
    sent = []
    for chunk in range(4):
        follow[chunk].wait()
        sums[...] = lax.dot_general(
            second[chunk * 256 : (chunk + 1) * 256, :],
            turned[...],
            (((1,), (1,)), ((), ())),
            preferred_element_type=jnp.float32,
        )
        span = slice(chunk * 16, (chunk + 1) * 16)
        for part in range(4):
            values = sums[:, part * 128 : (part + 1) * 128].astype(jnp.bfloat16)
            out[span, part] = values.reshape(16, 16, 128)
        rows = pl.ds(chunk * 16, 16)
        sent.append(pltpu.make_async_copy(out.at[rows], out_ref.at[rows], went.at[chunk]))
        sent[-1].start()
    for copy in sent:
        copy.wait()


def forward(x, first, twist, second):
    return pl.pallas_call(
        forward_kernel,
        out_shape=jax.ShapeDtypeStruct((64, 4, 16, 128), jnp.bfloat16),
        in_specs=[pl.BlockSpec(memory_space=NEAR)] * 3 + [pl.BlockSpec(memory_space=FAR)],
        out_specs=pl.BlockSpec(memory_space=FAR),
        scratch_shapes=[
            pltpu.VMEM((1024, 1024), jnp.bfloat16),
            pltpu.VMEM((512, 1024), jnp.bfloat16),
            pltpu.VMEM((256, 512), jnp.float32),
            pltpu.VMEM((64, 4, 16, 128), jnp.bfloat16),
            pltpu.SemaphoreType.DMA((4,)),
            pltpu.SemaphoreType.DMA((4,)),
        ],
        compiler_params=pltpu.CompilerParams(vmem_limit_bytes=49 * MIB),
        name="forward",
    )(x, first, twist, second)


def taps_kernel(band_ref, coef_ref, taps):
    lower = band_ref[1]
    width = band_ref[2]
    empty = jnp.zeros((TILE, TILE), jnp.bfloat16)
    taps[:TILE, 5 * TILE :] = empty
    taps[TILE:, :TILE] = empty
    for shift in range(WMAX):
        index = shift - HT - lower
        held = jnp.logical_and(index >= 0, index < width)
        weight = coef_ref[0, jnp.clip(index, 0, WMAX - 1)]
        scale = jnp.where(held, jnp.float32(1), jnp.float32(0))
        weight = (weight.astype(jnp.float32) * scale).astype(jnp.bfloat16)
        taps[:TILE, shift * TILE : (shift + 1) * TILE] = weight
        taps[TILE:, (shift + 1) * TILE : (shift + 2) * TILE] = weight


def tap_matrix(band, coef_table):
    return pl.pallas_call(
        taps_kernel,
        grid_spec=pltpu.PrefetchScalarGridSpec(
            num_scalar_prefetch=1,
            grid=(1,),
            in_specs=[pl.BlockSpec((1, WMAX, TILE, TILE), lambda i, band: (band[0], 0, 0, 0))],
            out_specs=pl.BlockSpec((256, 6 * TILE), lambda i, band: (0, 0)),
        ),
        out_shape=jax.ShapeDtypeStruct((256, 6 * TILE), jnp.bfloat16),
        compiler_params=pltpu.CompilerParams(vmem_limit_bytes=16 * MIB),
        cost_estimate=pl.CostEstimate(flops=2_000_000, bytes_accessed=600_000, transcendentals=0),
        name="taps",
    )(band, coef_table)


def migrate_kernel(spectrum_ref, taps, out_ref, padded, out, went):
    rim = jnp.zeros((HT * TILE, 2 * FB), jnp.bfloat16)
    padded[: HT * TILE, :] = rim
    padded[HT * TILE + R :, :] = rim
    for block in range(8):
        values = spectrum_ref[block * 32 : (block + 1) * 32].astype(jnp.float32)
        start = HT * TILE + block * 256
        for plane in range(2):
            rows = values[:, plane * ROWS : (plane + 1) * ROWS, :].reshape(256, FB)
            padded[start : start + 256, plane * FB : (plane + 1) * FB] = rows.astype(jnp.bfloat16)
    sent = []
    for block in range(8):
        moved = jnp.dot(
            taps[...], padded[block * 256 : block * 256 + 6 * TILE, :], preferred_element_type=jnp.float32
        )
        real = moved[:, :FB].reshape(32, ROWS, FB)
        imaginary = moved[:, FB:].reshape(32, ROWS, FB)
        out[block * 32 : (block + 1) * 32] = jnp.concatenate([real, imaginary], axis=1).astype(jnp.bfloat16)
        if block % 2 == 1:
            rows = pl.ds(block * 32 - 32, 64)
            sent.append(pltpu.make_async_copy(out.at[rows], out_ref.at[rows], went.at[block // 2]))
            sent[-1].start()
    for copy in sent:
        copy.wait()


def migrate(spectrum, taps):
    return pl.pallas_call(
        migrate_kernel,
        in_specs=[pl.BlockSpec(memory_space=NEAR)] * 2,
        out_specs=pl.BlockSpec(memory_space=FAR),
        scratch_shapes=[
            pltpu.VMEM((R + 2 * HT * TILE, 2 * FB), jnp.bfloat16),
            pltpu.VMEM((256, 16, 128), jnp.bfloat16),
            pltpu.SemaphoreType.DMA((4,)),
        ],
        out_shape=jax.ShapeDtypeStruct((256, 16, 128), jnp.bfloat16),
        compiler_params=pltpu.CompilerParams(vmem_limit_bytes=50 * MIB),
        name="migrate",
    )(spectrum, taps)


def rotor(turns):
    quarter = jnp.round(turns * 4.0)
    x = (turns - quarter * 0.25) * (2.0 * math.pi)
    square = x * x
    sine = x + x * square * (-1.0 / 6 + square * (1.0 / 120 + square * (-1.0 / 5040)))
    cosine = 1.0 + square * (-0.5 + square * (1.0 / 24 + square * (-1.0 / 720 + square * (1.0 / 40320))))
    count = quarter.astype(jnp.int32)
    swapped = (count & 1) == 1
    first = jnp.where(swapped, sine, cosine)
    second = jnp.where(swapped, cosine, sine)
    first = jnp.where(((count + 1) & 2) == 2, -first, first)
    second = jnp.where((count & 2) == 2, -second, second)
    return first, second


def phase_kernel(rate_ref, phase_ref):
    rate = rate_ref[...]
    lane = lax.broadcasted_iota(jnp.int32, (16, ROWS, FB), 2)
    step = lax.broadcasted_iota(jnp.int32, (16, ROWS, FB), 0)
    for chunk in range(4):
        for part in range(4):
            frequency = (step + chunk * 16) * P_SIZE + (lane + part * FB)
            signed = jnp.where(frequency >= A // 2, frequency - A, frequency).astype(jnp.float32)
            doppler = signed * (1.0 / A)
            cosine, sine = rotor(rate[None] * (doppler * doppler))
            phase_ref[0, chunk * 16 : (chunk + 1) * 16, part] = cosine
            phase_ref[1, chunk * 16 : (chunk + 1) * 16, part] = sine


def phases(rate):
    return pl.pallas_call(
        phase_kernel,
        out_shape=jax.ShapeDtypeStruct((2, 64, 4, ROWS, FB), jnp.float32),
        in_specs=[pl.BlockSpec(memory_space=NEAR)],
        out_specs=pl.BlockSpec(memory_space=NEAR),
        compiler_params=pltpu.CompilerParams(vmem_limit_bytes=16 * MIB),
        cost_estimate=pl.CostEstimate(flops=20_000_000, bytes_accessed=2_100_000, transcendentals=0),
        name="phases",
    )(rate)


def inverse_kernel(
    moved_ref,
    phase_ref,
    third_ref,
    last_ref,
    twist_ref,
    out_ref,
    third,
    last,
    twist,
    focused,
    turned,
    sums,
    stage,
    out,
    came,
    went,
):
    lead = fetch(third_ref, third, came.at[0], 4)
    turns = fetch(twist_ref.at[:2], twist, came.at[1], 1)
    follow = fetch(last_ref, last, came.at[2], 4)
    for copy in lead[:1] + turns + lead[1:] + follow:
        copy.start()
    for chunk in range(4):
        for part in range(4):
            span = slice(chunk * 16, (chunk + 1) * 16)
            cosine, sine = phase_ref[0, span, part], phase_ref[1, span, part]
            values = moved_ref[span, part].astype(jnp.float32)
            real, imaginary = values[:, :ROWS, :], values[:, ROWS:, :]
            both = jnp.concatenate(
                [real * cosine + imaginary * sine, imaginary * cosine - real * sine], axis=1
            ).astype(jnp.bfloat16)
            focused[chunk * 256 : (chunk + 1) * 256, part * FB : (part + 1) * FB] = both.reshape(256, FB)
    for chunk in range(4):
        lead[chunk].wait()
        if chunk == 0:
            turns[0].wait()
        sums[...] = jnp.dot(
            third[chunk * 256 : (chunk + 1) * 256, :], focused[...], preferred_element_type=jnp.float32
        )
        span = slice(chunk * 128, (chunk + 1) * 128)
        for part in range(4):
            lanes = slice(part * 128, (part + 1) * 128)
            real, imaginary = sums[:128, lanes], sums[128:, lanes]
            cosine, sine = twist[0, lanes, :], twist[1, lanes, :]
            turned[span, part * 128 : (part + 1) * 128] = (real * cosine - imaginary * sine).astype(jnp.bfloat16)
            turned[span, 512 + part * 128 : 640 + part * 128] = (imaginary * cosine + real * sine).astype(
                jnp.bfloat16
            )
    low = lax.broadcasted_iota(jnp.int32, (128, 128), 1) < HALF
    sent = []
    for chunk in range(4):
        follow[chunk].wait()
        sums[...] = lax.dot_general(
            last[chunk * 256 : (chunk + 1) * 256, :],
            turned[...],
            (((1,), (1,)), ((), ())),
            preferred_element_type=jnp.float32,
        )
        for pair in range(4):
            even = sums[:128, pair * 128 : (pair + 1) * 128]
            odd = sums[128:, pair * 128 : (pair + 1) * 128]
            stage[chunk % 2, pl.ds(2 * pair, 128, stride=8), :] = jnp.where(low, even, pltpu.roll(odd, HALF, 1))
            stage[chunk % 2, pl.ds(2 * pair + 1, 128, stride=8), :] = jnp.where(low, pltpu.roll(even, HALF, 1), odd)
        plane, base = chunk // 2, (chunk % 2) * 128
        for group in range(128):
            out[plane, :, (base + group) * 128 : (base + group + 1) * 128] = stage[
                chunk % 2, group * 8 : (group + 1) * 8, :
            ].astype(jnp.bfloat16)
        lanes = pl.ds(base * 128, A // 2)
        sent.append(pltpu.make_async_copy(out.at[plane, :, lanes], out_ref.at[plane, :, lanes], went.at[chunk]))
        sent[-1].start()
    for copy in sent:
        copy.wait()


def inverse(moved, phase, third, last, twist):
    return pl.pallas_call(
        inverse_kernel,
        out_shape=jax.ShapeDtypeStruct((2, ROWS, A), jnp.bfloat16),
        in_specs=[pl.BlockSpec(memory_space=NEAR)] * 2 + [pl.BlockSpec(memory_space=FAR)] * 3,
        out_specs=pl.BlockSpec(memory_space=FAR),
        scratch_shapes=[
            pltpu.VMEM((1024, 1024), jnp.bfloat16),
            pltpu.VMEM((1024, 1024), jnp.bfloat16),
            pltpu.VMEM((2, 512, 128), jnp.float32),
            pltpu.VMEM((1024, 512), jnp.bfloat16),
            pltpu.VMEM((512, 1024), jnp.bfloat16),
            pltpu.VMEM((256, 512), jnp.float32),
            pltpu.VMEM((2, 1024, 128), jnp.float32),
            pltpu.VMEM((2, ROWS, A), jnp.bfloat16),
            pltpu.SemaphoreType.DMA((3, 4)),
            pltpu.SemaphoreType.DMA((4,)),
        ],
        compiler_params=pltpu.CompilerParams(vmem_limit_bytes=50 * MIB),
        name="inverse",
    )(moved, phase, third, last, twist)


def body(echoes, coef_table, kern_id, band_lo, band_width, rate):
    ahead, behind = tables()
    az = lax.axis_index("az")
    block = lax.axis_index("rg") * lax.axis_size("az") + az
    band = jnp.stack([kern_id[block], band_lo[block], band_width[block]])
    rates = jnp.broadcast_to(lax.dynamic_slice(rate, (az * ROWS,), (ROWS,))[:, None], (ROWS, FB))
    piece = lax.all_to_all(pack(echoes), "az", 0, 0, tiled=True)
    spectrum = forward(piece.reshape(1024, 512), *ahead)
    spectrum = lax.all_to_all(spectrum.reshape(256, 16, 128), ("rg", "az"), 0, 0, tiled=True)
    moved = migrate(spectrum, tap_matrix(band, coef_table))
    moved = lax.all_to_all(moved, ("rg", "az"), 0, 0, tiled=True)
    return inverse(moved.reshape(64, 4, 16, 128), phases(rates), *behind)


def solution(mesh):
    in_specs = (P(None, "rg", "az"), P(), P(), P(), P(), P("rg"))
    out_specs = P(None, ("rg", "az"), None)
    return jax.shard_map(body, mesh=mesh, in_specs=in_specs, out_specs=out_specs, check_vma=False)
```

```python
import functools
import math

import jax
import jax.numpy as jnp
import ml_dtypes
import numpy as np
from jax import lax
from jax.experimental import pallas as pl
from jax.experimental.pallas import tpu as pltpu
from jax.sharding import PartitionSpec as P

A = 32768
P_SIZE = 512
Q = 64
R = 2048
TILE = 128
FB = 128
FBLK = 256
HT = 2
WMAX = 5
ROWS = 8
PACKS = 8
HALF = 64
MIB = 1024 * 1024
FAR = pltpu.MemorySpace.HBM
NEAR = pltpu.MemorySpace.VMEM


def angles(first, second, length):
    product = np.outer(np.arange(first), np.arange(second)) % length
    turn = product * (2.0 * math.pi / length)
    return np.cos(turn), np.sin(turn)


def rounded(values):
    return values.astype(np.float32).astype(ml_dtypes.bfloat16)


@functools.lru_cache(maxsize=None)
def tables():
    cosine, sine = angles(P_SIZE, P_SIZE, P_SIZE)
    cosine, sine = cosine / math.sqrt(P_SIZE), sine / math.sqrt(P_SIZE)
    whole = np.zeros((2, P_SIZE, 2, P_SIZE))
    whole[0, :, 0] = cosine
    whole[0, :, 1] = sine
    whole[1, :, 1] = cosine
    whole[1, :, 0] = -sine
    first = whole.reshape(2, 4, 128, 2, 64, 4, 2).transpose(1, 0, 2, 4, 6, 3, 5).reshape(1024, 1024)
    back = np.zeros((2, P_SIZE, 2, P_SIZE))
    back[0, :, 0] = cosine
    back[0, :, 1] = -sine
    back[1, :, 1] = cosine
    back[1, :, 0] = sine
    last = back.reshape(2, 2, 128, 2, 2, P_SIZE).transpose(0, 1, 3, 2, 4, 5).reshape(1024, 1024)
    cosine, sine = angles(Q, Q, Q)
    cosine, sine = cosine / math.sqrt(Q), sine / math.sqrt(Q)
    eye = np.eye(ROWS)
    small = np.zeros((2, Q, 2, Q))
    small[0, :, 0] = cosine
    small[0, :, 1] = sine
    small[1, :, 1] = cosine
    small[1, :, 0] = -sine
    second = np.einsum("pgqa,rs->gprqsa", small, eye).reshape(1024, 1024)
    small = np.zeros((2, Q, 2, Q))
    small[0, :, 0] = cosine
    small[0, :, 1] = -sine
    small[1, :, 1] = cosine
    small[1, :, 0] = sine
    third = np.einsum("paqg,rs->rpagqs", small, eye)
    third = third.reshape(4, 2, 2, Q, Q, 2, ROWS).transpose(0, 2, 1, 3, 4, 5, 6).reshape(1024, 1024)
    cosine, sine = angles(Q, P_SIZE, A)
    turned = np.stack([np.tile(part.T, (1, 2)) for part in (cosine, sine)]).astype(np.float32)
    straight = [np.tile(part, (2, 1)).reshape(128, 4, 128).transpose(1, 0, 2).reshape(512, 128) for part in (cosine, sine)]
    straight = np.concatenate([np.stack(straight), turned, turned, turned]).astype(np.float32)
    return (rounded(first), turned, rounded(second)), (rounded(third), rounded(last), straight)


def pack_kernel(echo_ref, out_ref, echo, stage, arrived):
    low = lax.broadcasted_iota(jnp.int32, (8, 128), 1) < HALF
    copies = []
    for step in range(PACKS):
        rows = pl.ds(step * (512 // PACKS), 512 // PACKS)
        copies.append(pltpu.make_async_copy(echo_ref.at[:, rows, :], echo.at[:, rows, :], arrived.at[step]))
        copies[-1].start()
    for dest in range(64):
        if dest % (64 // PACKS) == 0:
            copies[dest // (64 // PACKS)].wait()
        for plane in range(2):
            rows = echo[plane, dest * ROWS : (dest + 1) * ROWS, :].astype(jnp.float32)
            for part in range(4):
                stage[pl.ds((dest * 8 + plane * 4 + part) * 8, 8), :] = rows[:, part * 128 : (part + 1) * 128]
        for pair in range(4):
            even = stage[pl.ds(dest * 64 + 2 * pair, 8, stride=8), :]
            odd = stage[pl.ds(dest * 64 + 2 * pair + 1, 8, stride=8), :]
            lower = jnp.where(low, even, pltpu.roll(odd, HALF, 1))
            upper = jnp.where(low, pltpu.roll(even, HALF, 1), odd)
            both = jnp.concatenate([lower, upper], axis=0).astype(jnp.bfloat16)
            out_ref[dest, :, pair * 128 : (pair + 1) * 128] = both


def pack(echoes):
    return pl.pallas_call(
        pack_kernel,
        in_specs=[pl.BlockSpec(memory_space=FAR)],
        out_specs=pl.BlockSpec(memory_space=NEAR),
        out_shape=jax.ShapeDtypeStruct((64, 16, 512), jnp.bfloat16),
        scratch_shapes=[
            pltpu.VMEM((2, 512, 512), jnp.bfloat16),
            pltpu.VMEM((4096, 128), jnp.float32),
            pltpu.SemaphoreType.DMA((PACKS,)),
        ],
        compiler_params=pltpu.CompilerParams(vmem_limit_bytes=52 * MIB),
        name="pack",
    )(echoes)


def fetch(source, target, arrived, steps):
    copies = []
    rows = source.shape[0] // steps
    for step in range(steps):
        span = pl.ds(step * rows, rows)
        copies.append(pltpu.make_async_copy(source.at[span], target.at[span], arrived.at[step]))
    return copies


def forward_kernel(
    x_ref, first, twist, second_ref, out_ref, second, turned, sums, out, came, went
):
    follow = fetch(second_ref, second, came, 1)
    for copy in follow:
        copy.start()
    for chunk in range(4):
        sums[chunk % 2] = jnp.dot(
            first[chunk * 256 : (chunk + 1) * 256, :], x_ref[...], preferred_element_type=jnp.float32
        )
        span = slice(chunk * 128, (chunk + 1) * 128)
        cosine, sine = twist[0, span, :], twist[1, span, :]
        for pair in range(4):
            lanes = slice(pair * 128, (pair + 1) * 128)
            real, imaginary = sums[chunk % 2, :128, lanes], sums[chunk % 2, 128:, lanes]
            turned[span, pair * 128 : (pair + 1) * 128] = (real * cosine + imaginary * sine).astype(jnp.bfloat16)
            turned[span, 512 + pair * 128 : 640 + pair * 128] = (imaginary * cosine - real * sine).astype(
                jnp.bfloat16
            )
    follow[0].wait()
    sent = []
    for chunk in range(4):
        sums[chunk % 2] = lax.dot_general(
            second[chunk * 256 : (chunk + 1) * 256, :],
            turned[...],
            (((1,), (1,)), ((), ())),
            preferred_element_type=jnp.float32,
        )
        span = slice(chunk * 16, (chunk + 1) * 16)
        for part in range(4):
            values = sums[chunk % 2, :, part * 128 : (part + 1) * 128].astype(jnp.bfloat16)
            out[span, part] = values.reshape(16, 16, 128)
        if chunk % 2 == 1:
            rows = pl.ds(chunk * 16 - 16, 32)
            sent.append(pltpu.make_async_copy(out.at[rows], out_ref.at[rows], went.at[chunk // 2]))
            sent[-1].start()
    for copy in sent:
        copy.wait()


def forward(x, first, twist, second):
    return pl.pallas_call(
        forward_kernel,
        out_shape=jax.ShapeDtypeStruct((64, 4, 16, 128), jnp.bfloat16),
        in_specs=[pl.BlockSpec(memory_space=NEAR)] * 3 + [pl.BlockSpec(memory_space=FAR)],
        out_specs=pl.BlockSpec(memory_space=FAR),
        scratch_shapes=[
            pltpu.VMEM((1024, 1024), jnp.bfloat16),
            pltpu.VMEM((512, 1024), jnp.bfloat16),
            pltpu.VMEM((2, 256, 512), jnp.float32),
            pltpu.VMEM((64, 4, 16, 128), jnp.bfloat16),
            pltpu.SemaphoreType.DMA((1,)),
            pltpu.SemaphoreType.DMA((2,)),
        ],
        compiler_params=pltpu.CompilerParams(vmem_limit_bytes=49 * MIB),
        name="forward",
    )(x, first, twist, second)


def taps_kernel(band_ref, coef_ref, taps):
    lower = band_ref[1]
    width = band_ref[2]
    empty = jnp.zeros((TILE, TILE), jnp.bfloat16)
    taps[:TILE, 5 * TILE :] = empty
    taps[TILE:, :TILE] = empty
    for shift in range(WMAX):
        index = shift - HT - lower
        held = jnp.logical_and(index >= 0, index < width)
        weight = coef_ref[0, jnp.clip(index, 0, WMAX - 1)]
        scale = jnp.where(held, jnp.float32(1), jnp.float32(0))
        weight = (weight.astype(jnp.float32) * scale).astype(jnp.bfloat16)
        taps[:TILE, shift * TILE : (shift + 1) * TILE] = weight
        taps[TILE:, (shift + 1) * TILE : (shift + 2) * TILE] = weight


def tap_matrix(band, coef_table):
    return pl.pallas_call(
        taps_kernel,
        grid_spec=pltpu.PrefetchScalarGridSpec(
            num_scalar_prefetch=1,
            grid=(1,),
            in_specs=[pl.BlockSpec((1, WMAX, TILE, TILE), lambda i, band: (band[0], 0, 0, 0))],
            out_specs=pl.BlockSpec((256, 6 * TILE), lambda i, band: (0, 0)),
        ),
        out_shape=jax.ShapeDtypeStruct((256, 6 * TILE), jnp.bfloat16),
        compiler_params=pltpu.CompilerParams(vmem_limit_bytes=16 * MIB),
        cost_estimate=pl.CostEstimate(flops=2_000_000, bytes_accessed=600_000, transcendentals=0),
        name="taps",
    )(band, coef_table)


def migrate_kernel(spectrum_ref, taps, out_ref, padded, out, went):
    rim = jnp.zeros((HT * TILE, 2 * FB), jnp.bfloat16)
    padded[: HT * TILE, :] = rim
    padded[HT * TILE + R :, :] = rim
    for block in range(8):
        values = spectrum_ref[block * 32 : (block + 1) * 32].astype(jnp.float32)
        start = HT * TILE + block * 256
        for plane in range(2):
            rows = values[:, plane * ROWS : (plane + 1) * ROWS, :].reshape(256, FB)
            padded[start : start + 256, plane * FB : (plane + 1) * FB] = rows.astype(jnp.bfloat16)
    sent = []
    for block in range(8):
        moved = jnp.dot(
            taps[...], padded[block * 256 : block * 256 + 6 * TILE, :], preferred_element_type=jnp.float32
        )
        real = moved[:, :FB].reshape(32, ROWS, FB)
        imaginary = moved[:, FB:].reshape(32, ROWS, FB)
        out[block * 32 : (block + 1) * 32] = jnp.concatenate([real, imaginary], axis=1).astype(jnp.bfloat16)
        if block % 2 == 1:
            rows = pl.ds(block * 32 - 32, 64)
            sent.append(pltpu.make_async_copy(out.at[rows], out_ref.at[rows], went.at[block // 2]))
            sent[-1].start()
    for copy in sent:
        copy.wait()


def migrate(spectrum, taps):
    return pl.pallas_call(
        migrate_kernel,
        in_specs=[pl.BlockSpec(memory_space=NEAR)] * 2,
        out_specs=pl.BlockSpec(memory_space=FAR),
        scratch_shapes=[
            pltpu.VMEM((R + 2 * HT * TILE, 2 * FB), jnp.bfloat16),
            pltpu.VMEM((256, 16, 128), jnp.bfloat16),
            pltpu.SemaphoreType.DMA((4,)),
        ],
        out_shape=jax.ShapeDtypeStruct((256, 16, 128), jnp.bfloat16),
        compiler_params=pltpu.CompilerParams(vmem_limit_bytes=50 * MIB),
        name="migrate",
    )(spectrum, taps)


def rotor(turns):
    quarter = jnp.round(turns * 4.0)
    x = (turns - quarter * 0.25) * (2.0 * math.pi)
    square = x * x
    sine = x + x * square * (-1.0 / 6 + square * (1.0 / 120 + square * (-1.0 / 5040)))
    cosine = 1.0 + square * (-0.5 + square * (1.0 / 24 + square * (-1.0 / 720 + square * (1.0 / 40320))))
    count = quarter.astype(jnp.int32)
    swapped = (count & 1) == 1
    first = jnp.where(swapped, sine, cosine)
    second = jnp.where(swapped, cosine, sine)
    first = jnp.where(((count + 1) & 2) == 2, -first, first)
    second = jnp.where((count & 2) == 2, -second, second)
    return first, second


def phase_kernel(rate_ref, phase_ref):
    rate = rate_ref[...]
    lane = lax.broadcasted_iota(jnp.int32, (16, ROWS, FB), 2)
    step = lax.broadcasted_iota(jnp.int32, (16, ROWS, FB), 0)
    for chunk in range(4):
        for part in range(4):
            frequency = (step + chunk * 16) * P_SIZE + (lane + part * FB)
            signed = jnp.where(frequency >= A // 2, frequency - A, frequency).astype(jnp.float32)
            doppler = signed * (1.0 / A)
            cosine, sine = rotor(rate[None] * (doppler * doppler))
            phase_ref[0, chunk * 16 : (chunk + 1) * 16, part] = cosine
            phase_ref[1, chunk * 16 : (chunk + 1) * 16, part] = sine


def phases(rate):
    return pl.pallas_call(
        phase_kernel,
        out_shape=jax.ShapeDtypeStruct((2, 64, 4, ROWS, FB), jnp.float32),
        in_specs=[pl.BlockSpec(memory_space=NEAR)],
        out_specs=pl.BlockSpec(memory_space=NEAR),
        compiler_params=pltpu.CompilerParams(vmem_limit_bytes=16 * MIB),
        cost_estimate=pl.CostEstimate(flops=20_000_000, bytes_accessed=2_100_000, transcendentals=0),
        name="phases",
    )(rate)


def inverse_kernel(
    moved_ref,
    phase_ref,
    third_ref,
    last_ref,
    twist_ref,
    out_ref,
    third,
    last,
    twist,
    focused,
    turned,
    sums,
    stage,
    out,
    came,
    went,
):
    lead = fetch(third_ref, third, came.at[0], 1)
    turns = fetch(twist_ref.at[:2], twist, came.at[1], 1)
    follow = fetch(last_ref, last, came.at[2], 1)
    for copy in lead + turns + follow:
        copy.start()
    for chunk in range(4):
        for part in range(4):
            span = slice(chunk * 16, (chunk + 1) * 16)
            cosine, sine = phase_ref[0, span, part], phase_ref[1, span, part]
            values = moved_ref[span, part].astype(jnp.float32)
            real, imaginary = values[:, :ROWS, :], values[:, ROWS:, :]
            both = jnp.concatenate(
                [real * cosine + imaginary * sine, imaginary * cosine - real * sine], axis=1
            ).astype(jnp.bfloat16)
            focused[chunk * 256 : (chunk + 1) * 256, part * FB : (part + 1) * FB] = both.reshape(256, FB)
    lead[0].wait()
    turns[0].wait()
    for chunk in range(4):
        sums[chunk % 2] = jnp.dot(
            third[chunk * 256 : (chunk + 1) * 256, :], focused[...], preferred_element_type=jnp.float32
        )
        span = slice(chunk * 128, (chunk + 1) * 128)
        for part in range(4):
            lanes = slice(part * 128, (part + 1) * 128)
            real, imaginary = sums[chunk % 2, :128, lanes], sums[chunk % 2, 128:, lanes]
            cosine, sine = twist[0, lanes, :], twist[1, lanes, :]
            turned[span, part * 128 : (part + 1) * 128] = (real * cosine - imaginary * sine).astype(jnp.bfloat16)
            turned[span, 512 + part * 128 : 640 + part * 128] = (imaginary * cosine + real * sine).astype(
                jnp.bfloat16
            )
    low = lax.broadcasted_iota(jnp.int32, (128, 128), 1) < HALF
    follow[0].wait()
    sent = []
    for chunk in range(4):
        sums[chunk % 2] = lax.dot_general(
            last[chunk * 256 : (chunk + 1) * 256, :],
            turned[...],
            (((1,), (1,)), ((), ())),
            preferred_element_type=jnp.float32,
        )
        for pair in range(4):
            even = sums[chunk % 2, :128, pair * 128 : (pair + 1) * 128]
            odd = sums[chunk % 2, 128:, pair * 128 : (pair + 1) * 128]
            stage[chunk % 2, pl.ds(2 * pair, 128, stride=8), :] = jnp.where(low, even, pltpu.roll(odd, HALF, 1))
            stage[chunk % 2, pl.ds(2 * pair + 1, 128, stride=8), :] = jnp.where(low, pltpu.roll(even, HALF, 1), odd)
        plane, base = chunk // 2, (chunk % 2) * 128
        for group in range(128):
            out[plane, :, (base + group) * 128 : (base + group + 1) * 128] = stage[
                chunk % 2, group * 8 : (group + 1) * 8, :
            ].astype(jnp.bfloat16)
        if chunk % 2 == 1:
            sent.append(pltpu.make_async_copy(out.at[plane], out_ref.at[plane], went.at[plane]))
            sent[-1].start()
    for copy in sent:
        copy.wait()


def inverse(moved, phase, third, last, twist):
    return pl.pallas_call(
        inverse_kernel,
        out_shape=jax.ShapeDtypeStruct((2, ROWS, A), jnp.bfloat16),
        in_specs=[pl.BlockSpec(memory_space=NEAR)] * 2 + [pl.BlockSpec(memory_space=FAR)] * 3,
        out_specs=pl.BlockSpec(memory_space=FAR),
        scratch_shapes=[
            pltpu.VMEM((1024, 1024), jnp.bfloat16),
            pltpu.VMEM((1024, 1024), jnp.bfloat16),
            pltpu.VMEM((2, 512, 128), jnp.float32),
            pltpu.VMEM((1024, 512), jnp.bfloat16),
            pltpu.VMEM((512, 1024), jnp.bfloat16),
            pltpu.VMEM((2, 256, 512), jnp.float32),
            pltpu.VMEM((2, 1024, 128), jnp.float32),
            pltpu.VMEM((2, ROWS, A), jnp.bfloat16),
            pltpu.SemaphoreType.DMA((3, 1)),
            pltpu.SemaphoreType.DMA((2,)),
        ],
        compiler_params=pltpu.CompilerParams(vmem_limit_bytes=50 * MIB),
        name="inverse",
    )(moved, phase, third, last, twist)


def body(echoes, coef_table, kern_id, band_lo, band_width, rate):
    ahead, behind = tables()
    az = lax.axis_index("az")
    block = lax.axis_index("rg") * lax.axis_size("az") + az
    band = jnp.stack([kern_id[block], band_lo[block], band_width[block]])
    rates = jnp.broadcast_to(lax.dynamic_slice(rate, (az * ROWS,), (ROWS,))[:, None], (ROWS, FB))
    piece = lax.all_to_all(pack(echoes), "az", 0, 0, tiled=True)
    spectrum = forward(piece.reshape(1024, 512), *ahead)
    spectrum = lax.all_to_all(spectrum.reshape(256, 16, 128), ("rg", "az"), 0, 0, tiled=True)
    moved = migrate(spectrum, tap_matrix(band, coef_table))
    moved = lax.all_to_all(moved, ("rg", "az"), 0, 0, tiled=True)
    return inverse(moved.reshape(64, 4, 16, 128), phases(rates), *behind)


def solution(mesh):
    in_specs = (P(None, "rg", "az"), P(), P(), P(), P(), P("rg"))
    out_specs = P(None, ("rg", "az"), None)
    return jax.shard_map(body, mesh=mesh, in_specs=in_specs, out_specs=out_specs, check_vma=False)
```

```python
import functools
import math

import jax
import jax.numpy as jnp
import ml_dtypes
import numpy as np
from jax import lax
from jax.experimental import pallas as pl
from jax.experimental.pallas import tpu as pltpu
from jax.sharding import PartitionSpec as P

A = 32768
P_SIZE = 512
Q = 64
R = 2048
TILE = 128
FB = 128
FBLK = 256
HT = 2
WMAX = 5
ROWS = 8
PACKS = 2
HALF = 64
MIB = 1024 * 1024
FAR = pltpu.MemorySpace.HBM
NEAR = pltpu.MemorySpace.VMEM


def angles(first, second, length):
    product = np.outer(np.arange(first), np.arange(second)) % length
    turn = product * (2.0 * math.pi / length)
    return np.cos(turn), np.sin(turn)


def rounded(values):
    return values.astype(np.float32).astype(ml_dtypes.bfloat16)


@functools.lru_cache(maxsize=None)
def tables():
    cosine, sine = angles(P_SIZE, P_SIZE, P_SIZE)
    cosine, sine = cosine / math.sqrt(P_SIZE), sine / math.sqrt(P_SIZE)
    whole = np.zeros((2, P_SIZE, 2, P_SIZE))
    whole[0, :, 0] = cosine
    whole[0, :, 1] = sine
    whole[1, :, 1] = cosine
    whole[1, :, 0] = -sine
    first = whole.reshape(2, 4, 128, 2, 64, 4, 2).transpose(1, 0, 2, 4, 6, 3, 5).reshape(1024, 1024)
    back = np.zeros((2, P_SIZE, 2, P_SIZE))
    back[0, :, 0] = cosine
    back[0, :, 1] = -sine
    back[1, :, 1] = cosine
    back[1, :, 0] = sine
    last = back.reshape(2, 2, 128, 2, 2, P_SIZE).transpose(0, 1, 3, 2, 4, 5).reshape(1024, 1024)
    cosine, sine = angles(Q, Q, Q)
    cosine, sine = cosine / math.sqrt(Q), sine / math.sqrt(Q)
    eye = np.eye(ROWS)
    small = np.zeros((2, Q, 2, Q))
    small[0, :, 0] = cosine
    small[0, :, 1] = sine
    small[1, :, 1] = cosine
    small[1, :, 0] = -sine
    second = np.einsum("pgqa,rs->gprqsa", small, eye).reshape(1024, 1024)
    small = np.zeros((2, Q, 2, Q))
    small[0, :, 0] = cosine
    small[0, :, 1] = -sine
    small[1, :, 1] = cosine
    small[1, :, 0] = sine
    third = np.einsum("paqg,rs->rpagqs", small, eye)
    third = third.reshape(4, 2, 2, Q, Q, 2, ROWS).transpose(0, 2, 1, 3, 4, 5, 6).reshape(1024, 1024)
    cosine, sine = angles(Q, P_SIZE, A)
    turned = np.stack([np.tile(part.T, (1, 2)) for part in (cosine, sine)]).astype(np.float32)
    straight = [np.tile(part, (2, 1)).reshape(128, 4, 128).transpose(1, 0, 2).reshape(512, 128) for part in (cosine, sine)]
    straight = np.concatenate([np.stack(straight), turned, turned, turned]).astype(np.float32)
    return (rounded(first), turned, rounded(second)), (rounded(third), rounded(last), straight)


def pack_kernel(echo_ref, out_ref, echo, stage, arrived):
    low = lax.broadcasted_iota(jnp.int32, (8, 128), 1) < HALF
    copies = []
    for step in range(PACKS):
        rows = pl.ds(step * (512 // PACKS), 512 // PACKS)
        copies.append(pltpu.make_async_copy(echo_ref.at[:, rows, :], echo.at[:, rows, :], arrived.at[step]))
        copies[-1].start()
    for dest in range(64):
        if dest % (64 // PACKS) == 0:
            copies[dest // (64 // PACKS)].wait()
        for plane in range(2):
            rows = echo[plane, dest * ROWS : (dest + 1) * ROWS, :].astype(jnp.float32)
            for part in range(4):
                stage[pl.ds((dest * 8 + plane * 4 + part) * 8, 8), :] = rows[:, part * 128 : (part + 1) * 128]
        for pair in range(4):
            even = stage[pl.ds(dest * 64 + 2 * pair, 8, stride=8), :]
            odd = stage[pl.ds(dest * 64 + 2 * pair + 1, 8, stride=8), :]
            lower = jnp.where(low, even, pltpu.roll(odd, HALF, 1))
            upper = jnp.where(low, pltpu.roll(even, HALF, 1), odd)
            both = jnp.concatenate([lower, upper], axis=0).astype(jnp.bfloat16)
            out_ref[dest, :, pair * 128 : (pair + 1) * 128] = both


def pack(echoes):
    return pl.pallas_call(
        pack_kernel,
        in_specs=[pl.BlockSpec(memory_space=FAR)],
        out_specs=pl.BlockSpec(memory_space=NEAR),
        out_shape=jax.ShapeDtypeStruct((64, 16, 512), jnp.bfloat16),
        scratch_shapes=[
            pltpu.VMEM((2, 512, 512), jnp.bfloat16),
            pltpu.VMEM((4096, 128), jnp.float32),
            pltpu.SemaphoreType.DMA((PACKS,)),
        ],
        compiler_params=pltpu.CompilerParams(vmem_limit_bytes=52 * MIB),
        name="pack",
    )(echoes)


def fetch(source, target, arrived, steps):
    copies = []
    rows = source.shape[0] // steps
    for step in range(steps):
        span = pl.ds(step * rows, rows)
        copies.append(pltpu.make_async_copy(source.at[span], target.at[span], arrived.at[step]))
    return copies


def forward_kernel(
    x_ref, first, twist, second_ref, out_ref, second, turned, sums, out, came, went
):
    follow = fetch(second_ref, second, came, 1)
    for copy in follow:
        copy.start()
    for chunk in range(4):
        sums[chunk % 2] = jnp.dot(
            first[chunk * 256 : (chunk + 1) * 256, :], x_ref[...], preferred_element_type=jnp.float32
        )
        span = slice(chunk * 128, (chunk + 1) * 128)
        cosine, sine = twist[0, span, :], twist[1, span, :]
        for pair in range(4):
            lanes = slice(pair * 128, (pair + 1) * 128)
            real, imaginary = sums[chunk % 2, :128, lanes], sums[chunk % 2, 128:, lanes]
            turned[span, pair * 128 : (pair + 1) * 128] = (real * cosine + imaginary * sine).astype(jnp.bfloat16)
            turned[span, 512 + pair * 128 : 640 + pair * 128] = (imaginary * cosine - real * sine).astype(
                jnp.bfloat16
            )
    follow[0].wait()
    sent = []
    for chunk in range(4):
        sums[chunk % 2] = lax.dot_general(
            second[chunk * 256 : (chunk + 1) * 256, :],
            turned[...],
            (((1,), (1,)), ((), ())),
            preferred_element_type=jnp.float32,
        )
        span = slice(chunk * 16, (chunk + 1) * 16)
        for part in range(4):
            values = sums[chunk % 2, :, part * 128 : (part + 1) * 128].astype(jnp.bfloat16)
            out[span, part] = values.reshape(16, 16, 128)
        if chunk % 2 == 1:
            rows = pl.ds(chunk * 16 - 16, 32)
            sent.append(pltpu.make_async_copy(out.at[rows], out_ref.at[rows], went.at[chunk // 2]))
            sent[-1].start()
    for copy in sent:
        copy.wait()


def forward(x, first, twist, second):
    return pl.pallas_call(
        forward_kernel,
        out_shape=jax.ShapeDtypeStruct((64, 4, 16, 128), jnp.bfloat16),
        in_specs=[pl.BlockSpec(memory_space=NEAR)] * 3 + [pl.BlockSpec(memory_space=FAR)],
        out_specs=pl.BlockSpec(memory_space=FAR),
        scratch_shapes=[
            pltpu.VMEM((1024, 1024), jnp.bfloat16),
            pltpu.VMEM((512, 1024), jnp.bfloat16),
            pltpu.VMEM((2, 256, 512), jnp.float32),
            pltpu.VMEM((64, 4, 16, 128), jnp.bfloat16),
            pltpu.SemaphoreType.DMA((1,)),
            pltpu.SemaphoreType.DMA((2,)),
        ],
        compiler_params=pltpu.CompilerParams(vmem_limit_bytes=49 * MIB),
        name="forward",
    )(x, first, twist, second)


def taps_kernel(band_ref, coef_ref, taps):
    lower = band_ref[1]
    width = band_ref[2]
    empty = jnp.zeros((TILE, TILE), jnp.bfloat16)
    taps[:TILE, 5 * TILE :] = empty
    taps[TILE:, :TILE] = empty
    for shift in range(WMAX):
        index = shift - HT - lower
        held = jnp.logical_and(index >= 0, index < width)
        weight = coef_ref[0, jnp.clip(index, 0, WMAX - 1)]
        scale = jnp.where(held, jnp.float32(1), jnp.float32(0))
        weight = (weight.astype(jnp.float32) * scale).astype(jnp.bfloat16)
        taps[:TILE, shift * TILE : (shift + 1) * TILE] = weight
        taps[TILE:, (shift + 1) * TILE : (shift + 2) * TILE] = weight


def tap_matrix(band, coef_table):
    return pl.pallas_call(
        taps_kernel,
        grid_spec=pltpu.PrefetchScalarGridSpec(
            num_scalar_prefetch=1,
            grid=(1,),
            in_specs=[pl.BlockSpec((1, WMAX, TILE, TILE), lambda i, band: (band[0], 0, 0, 0))],
            out_specs=pl.BlockSpec((256, 6 * TILE), lambda i, band: (0, 0)),
        ),
        out_shape=jax.ShapeDtypeStruct((256, 6 * TILE), jnp.bfloat16),
        compiler_params=pltpu.CompilerParams(vmem_limit_bytes=16 * MIB),
        cost_estimate=pl.CostEstimate(flops=2_000_000, bytes_accessed=600_000, transcendentals=0),
        name="taps",
    )(band, coef_table)


def migrate_kernel(spectrum_ref, taps, out_ref, padded, out, went):
    rim = jnp.zeros((HT * TILE, 2 * FB), jnp.bfloat16)
    padded[: HT * TILE, :] = rim
    padded[HT * TILE + R :, :] = rim
    for block in range(8):
        values = spectrum_ref[block * 32 : (block + 1) * 32].astype(jnp.float32)
        start = HT * TILE + block * 256
        for plane in range(2):
            rows = values[:, plane * ROWS : (plane + 1) * ROWS, :].reshape(256, FB)
            padded[start : start + 256, plane * FB : (plane + 1) * FB] = rows.astype(jnp.bfloat16)
    sent = []
    for block in range(8):
        moved = jnp.dot(
            taps[...], padded[block * 256 : block * 256 + 6 * TILE, :], preferred_element_type=jnp.float32
        )
        real = moved[:, :FB].reshape(32, ROWS, FB)
        imaginary = moved[:, FB:].reshape(32, ROWS, FB)
        out[block * 32 : (block + 1) * 32] = jnp.concatenate([real, imaginary], axis=1).astype(jnp.bfloat16)
        if block % 2 == 1:
            rows = pl.ds(block * 32 - 32, 64)
            sent.append(pltpu.make_async_copy(out.at[rows], out_ref.at[rows], went.at[block // 2]))
            sent[-1].start()
    for copy in sent:
        copy.wait()


def migrate(spectrum, taps):
    return pl.pallas_call(
        migrate_kernel,
        in_specs=[pl.BlockSpec(memory_space=NEAR)] * 2,
        out_specs=pl.BlockSpec(memory_space=FAR),
        scratch_shapes=[
            pltpu.VMEM((R + 2 * HT * TILE, 2 * FB), jnp.bfloat16),
            pltpu.VMEM((256, 16, 128), jnp.bfloat16),
            pltpu.SemaphoreType.DMA((4,)),
        ],
        out_shape=jax.ShapeDtypeStruct((256, 16, 128), jnp.bfloat16),
        compiler_params=pltpu.CompilerParams(vmem_limit_bytes=50 * MIB),
        name="migrate",
    )(spectrum, taps)


def rotor(turns):
    quarter = jnp.round(turns * 4.0)
    x = (turns - quarter * 0.25) * (2.0 * math.pi)
    square = x * x
    sine = x + x * square * (-1.0 / 6 + square * (1.0 / 120 + square * (-1.0 / 5040)))
    cosine = 1.0 + square * (-0.5 + square * (1.0 / 24 + square * (-1.0 / 720 + square * (1.0 / 40320))))
    count = quarter.astype(jnp.int32)
    swapped = (count & 1) == 1
    first = jnp.where(swapped, sine, cosine)
    second = jnp.where(swapped, cosine, sine)
    first = jnp.where(((count + 1) & 2) == 2, -first, first)
    second = jnp.where((count & 2) == 2, -second, second)
    return first, second


def phase_kernel(rate_ref, phase_ref):
    rate = rate_ref[...]
    lane = lax.broadcasted_iota(jnp.int32, (16, ROWS, FB), 2)
    step = lax.broadcasted_iota(jnp.int32, (16, ROWS, FB), 0)
    for chunk in range(4):
        for part in range(4):
            frequency = (step + chunk * 16) * P_SIZE + (lane + part * FB)
            signed = jnp.where(frequency >= A // 2, frequency - A, frequency).astype(jnp.float32)
            doppler = signed * (1.0 / A)
            cosine, sine = rotor(rate[None] * (doppler * doppler))
            phase_ref[0, chunk * 16 : (chunk + 1) * 16, part] = cosine
            phase_ref[1, chunk * 16 : (chunk + 1) * 16, part] = sine


def phases(rate):
    return pl.pallas_call(
        phase_kernel,
        out_shape=jax.ShapeDtypeStruct((2, 64, 4, ROWS, FB), jnp.float32),
        in_specs=[pl.BlockSpec(memory_space=NEAR)],
        out_specs=pl.BlockSpec(memory_space=NEAR),
        compiler_params=pltpu.CompilerParams(vmem_limit_bytes=16 * MIB),
        cost_estimate=pl.CostEstimate(flops=20_000_000, bytes_accessed=2_100_000, transcendentals=0),
        name="phases",
    )(rate)


def inverse_kernel(
    moved_ref,
    phase_ref,
    third_ref,
    last_ref,
    twist_ref,
    out_ref,
    third,
    last,
    twist,
    focused,
    turned,
    sums,
    stage,
    out,
    came,
    went,
):
    lead = fetch(third_ref, third, came.at[0], 1)
    turns = fetch(twist_ref.at[:2], twist, came.at[1], 1)
    follow = fetch(last_ref, last, came.at[2], 1)
    for copy in lead + turns:
        copy.start()
    for chunk in range(4):
        for part in range(4):
            span = slice(chunk * 16, (chunk + 1) * 16)
            cosine, sine = phase_ref[0, span, part], phase_ref[1, span, part]
            values = moved_ref[span, part].astype(jnp.float32)
            real, imaginary = values[:, :ROWS, :], values[:, ROWS:, :]
            both = jnp.concatenate(
                [real * cosine + imaginary * sine, imaginary * cosine - real * sine], axis=1
            ).astype(jnp.bfloat16)
            focused[chunk * 256 : (chunk + 1) * 256, part * FB : (part + 1) * FB] = both.reshape(256, FB)
    lead[0].wait()
    turns[0].wait()
    follow[0].start()
    for chunk in range(4):
        sums[chunk % 2] = jnp.dot(
            third[chunk * 256 : (chunk + 1) * 256, :], focused[...], preferred_element_type=jnp.float32
        )
        span = slice(chunk * 128, (chunk + 1) * 128)
        for part in range(4):
            lanes = slice(part * 128, (part + 1) * 128)
            real, imaginary = sums[chunk % 2, :128, lanes], sums[chunk % 2, 128:, lanes]
            cosine, sine = twist[0, lanes, :], twist[1, lanes, :]
            turned[span, part * 128 : (part + 1) * 128] = (real * cosine - imaginary * sine).astype(jnp.bfloat16)
            turned[span, 512 + part * 128 : 640 + part * 128] = (imaginary * cosine + real * sine).astype(
                jnp.bfloat16
            )
    low = lax.broadcasted_iota(jnp.int32, (128, 128), 1) < HALF
    follow[0].wait()
    sent = []
    for chunk in range(4):
        sums[chunk % 2] = lax.dot_general(
            last[chunk * 256 : (chunk + 1) * 256, :],
            turned[...],
            (((1,), (1,)), ((), ())),
            preferred_element_type=jnp.float32,
        )
        for pair in range(4):
            even = sums[chunk % 2, :128, pair * 128 : (pair + 1) * 128]
            odd = sums[chunk % 2, 128:, pair * 128 : (pair + 1) * 128]
            stage[chunk % 2, pl.ds(2 * pair, 128, stride=8), :] = jnp.where(low, even, pltpu.roll(odd, HALF, 1))
            stage[chunk % 2, pl.ds(2 * pair + 1, 128, stride=8), :] = jnp.where(low, pltpu.roll(even, HALF, 1), odd)
        plane, base = chunk // 2, (chunk % 2) * 128
        for group in range(128):
            out[plane, :, (base + group) * 128 : (base + group + 1) * 128] = stage[
                chunk % 2, group * 8 : (group + 1) * 8, :
            ].astype(jnp.bfloat16)
        if chunk % 2 == 1:
            sent.append(pltpu.make_async_copy(out.at[plane], out_ref.at[plane], went.at[plane]))
            sent[-1].start()
    for copy in sent:
        copy.wait()


def inverse(moved, phase, third, last, twist):
    return pl.pallas_call(
        inverse_kernel,
        out_shape=jax.ShapeDtypeStruct((2, ROWS, A), jnp.bfloat16),
        in_specs=[pl.BlockSpec(memory_space=NEAR)] * 2 + [pl.BlockSpec(memory_space=FAR)] * 3,
        out_specs=pl.BlockSpec(memory_space=FAR),
        scratch_shapes=[
            pltpu.VMEM((1024, 1024), jnp.bfloat16),
            pltpu.VMEM((1024, 1024), jnp.bfloat16),
            pltpu.VMEM((2, 512, 128), jnp.float32),
            pltpu.VMEM((1024, 512), jnp.bfloat16),
            pltpu.VMEM((512, 1024), jnp.bfloat16),
            pltpu.VMEM((2, 256, 512), jnp.float32),
            pltpu.VMEM((2, 1024, 128), jnp.float32),
            pltpu.VMEM((2, ROWS, A), jnp.bfloat16),
            pltpu.SemaphoreType.DMA((3, 1)),
            pltpu.SemaphoreType.DMA((2,)),
        ],
        compiler_params=pltpu.CompilerParams(vmem_limit_bytes=50 * MIB),
        name="inverse",
    )(moved, phase, third, last, twist)


def body(echoes, coef_table, kern_id, band_lo, band_width, rate):
    ahead, behind = tables()
    az = lax.axis_index("az")
    block = lax.axis_index("rg") * lax.axis_size("az") + az
    band = jnp.stack([kern_id[block], band_lo[block], band_width[block]])
    rates = jnp.broadcast_to(lax.dynamic_slice(rate, (az * ROWS,), (ROWS,))[:, None], (ROWS, FB))
    piece = lax.all_to_all(pack(echoes), "az", 0, 0, tiled=True)
    spectrum = forward(piece.reshape(1024, 512), *ahead)
    spectrum = lax.all_to_all(spectrum.reshape(256, 16, 128), ("rg", "az"), 0, 0, tiled=True)
    moved = migrate(spectrum, tap_matrix(band, coef_table))
    moved = lax.all_to_all(moved, ("rg", "az"), 0, 0, tiled=True)
    return inverse(moved.reshape(64, 4, 16, 128), phases(rates), *behind)


def solution(mesh):
    in_specs = (P(None, "rg", "az"), P(), P(), P(), P(), P("rg"))
    out_specs = P(None, ("rg", "az"), None)
    return jax.shard_map(body, mesh=mesh, in_specs=in_specs, out_specs=out_specs, check_vma=False)
```
